256 devices in a mesh: dp: 16 (over y, x), seq: 16 (over z, core).
Axes of the slice: x: 4, y: 4, z: 8, core: 2. Of those that a mesh axis runs over, the one named last changes fastest.
Arguments:
- ssm_input: bfloat16 [16, 2048, 2048], P('dp', 'seq'), may hold values from -6 to 6
- gate_input: bfloat16 [16, 2048, 2048], P('dp', 'seq'), may hold values from -6 to 6
- grad_gated: bfloat16 [16, 2048, 2048], P('dp', 'seq'), may hold values from -6 to 6
- x_proj: bfloat16 [2048, 96], replicated, may hold values from -0.125 to 0.125
- dt_proj: bfloat16 [64, 2048], replicated, may hold values from -0.75 to 0.75
- dt_bias: float32 [2048], replicated, may hold values from -14 to -2
- fid_bias: float32 [2, 2048], replicated, may hold values from -3 to 3
- a_log: float32 [2048, 16], replicated, may hold values from 0 to 2.77
- skip_gain: float32 [2048], replicated, may hold values from 0.5 to 1.5
- rec_lengths: int32 [16], P('dp'), may hold values from 512 to 2048, as said below
- fid_labels: int32 [16], P('dp'), may hold values from 0 to 1
Outputs:
- gated: bfloat16 [16, 2048, 2048], P('dp', 'seq')
- grad_input: bfloat16 [16, 2048, 2048], P('dp', 'seq')
- grad_gate: bfloat16 [16, 2048, 2048], P('dp', 'seq')
- grad_x_proj: float32 [2048, 96], P('dp')
- grad_dt_proj: float32 [64, 2048], P(None, 'dp')
- grad_a_log: float32 [2048, 16], P('dp')
- grad_skip: float32 [2048], P('dp')
- grad_dt_bias: float32 [2048], P('dp')
- grad_fid_bias: float32 [2, 2048], P(None, 'dp')
The draws below stay inside these ranges and needn't reach their ends.
Inputs may be any that keep to these rules, and one draw needn't show every extreme that they name: `rec_lengths`: each record's count of valid time steps; in every draw some record is 2048 long.
All inputs are finite; a program needn't handle non-finite values.
Results may differ from the reference program's by a relative error of at most 0.0068.
Values sent between devices are 32-bit elements; how exact they have to be, the bound alone decides.
A program may use at most 64 MiB of HBM per device.

```python
import jax
import jax.numpy as jnp
from jax import lax

INNER = 2048
RANK = 64
STATES = 16
KINDS = 2
SEG_DEV = 128
RECORDS = 16
LENGTH = 2048


def draw_ssm_input(key, part):
    key_rough, key_offset = jax.random.split(key, 2)
    offset = jax.random.normal(key_offset, (RECORDS, 1, INNER), jnp.float32)
    rough = jax.random.normal(key_rough, (RECORDS, LENGTH, INNER), jnp.float32)
    result = rough + offset
    return jnp.clip(result, -6.0, 6.0).astype(jnp.bfloat16)


def draw_dt_bias(key, part):
    key_kind, key_slow, key_fast = jax.random.split(key, 3)
    slow_share = 0.5
    slow = jax.random.uniform(key_kind, (INNER,), jnp.float32) < slow_share
    slow_step = jnp.exp(jax.random.uniform(key_slow, (INNER,), jnp.float32, jnp.log(0.05), jnp.log(0.15))) / LENGTH
    fast_step = jnp.exp(jax.random.uniform(key_fast, (INNER,), jnp.float32, jnp.log(0.01), jnp.log(0.1)))
    stepsize = jnp.where(slow, slow_step, fast_step)
    return jnp.log(jnp.expm1(stepsize)).astype(jnp.float32)


def draw_rec_lengths(key, part):
    key_all, key_full = jax.random.split(key)
    lengths = jax.random.randint(key_all, (RECORDS,), LENGTH // 4, LENGTH + 1, dtype=jnp.int32)
    chosen = jax.random.randint(key_full, (), 0, RECORDS, dtype=jnp.int32)
    return jnp.where(jnp.arange(RECORDS, dtype=jnp.int32) == chosen, LENGTH, lengths).astype(jnp.int32)


def with_ends(values, rng, smallest, high):
    place = [jax.random.randint(jax.random.fold_in(rng, axis), (), 0, length) for axis, length in enumerate(values.shape)]
    widest = values.shape.index(max(values.shape))
    neighbour = place[:widest] + [(place[widest] + 1) % values.shape[widest]] + place[widest + 1:]
    return values.at[tuple(place)].set(smallest).at[tuple(neighbour)].set(high)


def shard_levels(stream_key, dims, cuts, low, high):
    gain, own = 1.0, jax.random.fold_in(stream_key, 6)
    for dim, blocks in cuts:
        heights = jnp.exp(jax.random.uniform(jax.random.fold_in(own, dim), (blocks,), jnp.float32, low / len(cuts), high / len(cuts)))
        gain = gain * jnp.repeat(heights, dims[dim] // blocks).reshape([-1 if axis == dim else 1 for axis in range(len(dims))])
    return gain


def centred(own_key, extent, spread, reach, shards=(), kind=jnp.bfloat16):
    loudness = shard_levels(own_key, extent, shards, -0.22, 0.18) if shards else 1.0
    entries = jax.random.normal(own_key, extent, jnp.float32) * spread * loudness
    return jnp.minimum(jnp.maximum(entries, -reach), reach).astype(kind)


def setup_inputs(seed: int = 0) -> dict:
    streams_of = jax.random.split(jax.random.key(seed), 12)
    ssm_input = draw_ssm_input(jax.random.fold_in(streams_of[11], 71), 0)
    gate_input = centred(streams_of[1], (RECORDS, LENGTH, INNER), 1.0, 6.0, ((0, 16), (1, 16)))
    grad_gated = centred(streams_of[2], (RECORDS, LENGTH, INNER), 1.0, 6.0, ((0, 16), (1, 16)))
    x_proj = centred(streams_of[3], (INNER, RANK + 2 * STATES), INNER ** -0.5, 0.125)
    dt_proj = centred(streams_of[4], (RANK, INNER), RANK ** -0.5, 0.75)
    dt_bias = draw_dt_bias(jax.random.fold_in(streams_of[11], 71), 0)
    fid_bias = centred(streams_of[6], (KINDS, INNER), 0.5, 3.0, (), jnp.float32)
    a_log = jnp.clip(jax.random.uniform(streams_of[7], (INNER, STATES), jnp.float32, 0.0, 2.77), 0.0, 2.77)
    skip_gain = jnp.clip(jax.random.uniform(streams_of[8], (INNER,), jnp.float32, 0.5, 1.5), 0.5, 1.5)
    rec_lengths = draw_rec_lengths(jax.random.fold_in(streams_of[11], 71), 0)
    fid_labels = with_ends(jax.random.randint(streams_of[10], (RECORDS,), 0, KINDS), jax.random.fold_in(streams_of[10], 1), 0, KINDS - 1).astype(jnp.int32)
    return dict(ssm_input=ssm_input, gate_input=gate_input, grad_gated=grad_gated, x_proj=x_proj, dt_proj=dt_proj, dt_bias=dt_bias, fid_bias=fid_bias, a_log=a_log, skip_gain=skip_gain, rec_lengths=rec_lengths, fid_labels=fid_labels)


def pair_scan(earlier, latter):
    decay_early, drive_early = earlier
    decay_late, drive_late = latter
    return (decay_early * decay_late, decay_late * drive_early + drive_late)

def scan_record(stepsize, b_proj, c_proj, values, a_matrix, h_start):
    decay = jnp.exp(stepsize[:, :, None] * a_matrix[None, :, :])
    drive = (stepsize * values)[:, :, None] * b_proj[:, None, :]
    drive = drive.at[0].add(decay[0] * h_start)
    _, states = lax.associative_scan(pair_scan, (decay, drive), axis=0)
    return (jnp.einsum('ken,kn->ke', states, c_proj), states[-1])

def scan_blocks(stepsize, b_proj, c_proj, values, a_matrix):
    count = LENGTH // SEG_DEV

    def one_block(h_now, pieces):
        step_blk, b_blk, c_blk, val_blk = pieces
        y_part, h_next = scan_record(step_blk, b_blk, c_blk, val_blk, a_matrix, h_now)
        return (h_next, y_part)
    pieces = tuple((p.reshape((count, SEG_DEV) + p.shape[1:]) for p in (stepsize, b_proj, c_proj, values)))
    h_zero = jnp.zeros((INNER, STATES), jnp.float32)
    _, ys = lax.scan(jax.checkpoint(one_block), h_zero, pieces)
    return ys.reshape((LENGTH, INNER))

def reference(ssm_input, gate_input, grad_gated, x_proj, dt_proj, dt_bias, fid_bias, a_log, skip_gain, rec_lengths, fid_labels):
    a_matrix = -jnp.exp(a_log)
    onehot = (fid_labels[:, None] == jnp.arange(KINDS, dtype=jnp.int32)[None, :]).astype(jnp.float32)

    def per_record(pieces):
        u_rec, gate_rec, out_rec, rec_length, kind_row = pieces
        values = u_rec.astype(jnp.float32)
        projected = jnp.dot(u_rec, x_proj, preferred_element_type=jnp.float32)
        low = projected[:, :RANK].astype(jnp.bfloat16)
        b_proj = projected[:, RANK:RANK + STATES]
        c_proj = projected[:, RANK + STATES:]
        dt_raw = jnp.dot(low, dt_proj, preferred_element_type=jnp.float32) + dt_bias + jnp.dot(kind_row, fid_bias, precision=lax.Precision.HIGHEST)
        live = (jnp.arange(LENGTH, dtype=jnp.int32) < rec_length).astype(jnp.float32)[:, None]
        stepsize = jax.nn.softplus(dt_raw) * live
        y_ssm, core_back = jax.vjp(scan_blocks, stepsize, b_proj, c_proj, values, a_matrix)
        y_full = y_ssm + skip_gain * values
        gate_value = gate_rec.astype(jnp.float32)
        gate_sigmoid = jax.nn.sigmoid(gate_value)
        gate_silu = gate_value * gate_sigmoid
        gated = (y_full * gate_silu * live).astype(jnp.bfloat16)
        out_grad = out_rec.astype(jnp.float32) * live
        y_grad = out_grad * gate_silu
        z_grad = out_grad * y_full * (gate_sigmoid * (1.0 + gate_value * (1.0 - gate_sigmoid)))
        step_grad, b_grad, c_grad, u_grad, a_grad = core_back(y_grad)
        dt_grad = step_grad * live * jax.nn.sigmoid(dt_raw)
        dt_grad_b = dt_grad.astype(jnp.bfloat16)
        g_dt_proj = jnp.dot(low.T, dt_grad_b, preferred_element_type=jnp.float32)
        low_grad = jnp.dot(dt_grad_b, dt_proj.T, preferred_element_type=jnp.float32)
        proj_grad = jnp.concatenate([low_grad, b_grad, c_grad], axis=1).astype(jnp.bfloat16)
        g_x_proj = jnp.dot(u_rec.T, proj_grad, preferred_element_type=jnp.float32)
        input_grad = u_grad + y_grad * skip_gain + jnp.dot(proj_grad, x_proj.T, preferred_element_type=jnp.float32)
        return (gated, input_grad.astype(jnp.bfloat16), z_grad.astype(jnp.bfloat16), g_x_proj, g_dt_proj, a_grad * a_matrix, lax.optimization_barrier(jnp.sum(y_grad * values, axis=0)), lax.optimization_barrier(jnp.sum(dt_grad, axis=0)))
    results = lax.map(per_record, (ssm_input, gate_input, grad_gated, rec_lengths, onehot))
    gated, grad_input, grad_gate, g_x_proj, g_dt_proj, g_a_log, g_skip, dt_sums = results
    grad_fid_bias = jnp.dot(onehot.T, dt_sums, precision=lax.Precision.HIGHEST)
    return (gated, grad_input, grad_gate, lax.optimization_barrier(jnp.sum(g_x_proj, axis=0)), lax.optimization_barrier(jnp.sum(g_dt_proj, axis=0)), lax.optimization_barrier(jnp.sum(g_a_log, axis=0)), lax.optimization_barrier(jnp.sum(g_skip, axis=0)), lax.optimization_barrier(jnp.sum(dt_sums, axis=0)), grad_fid_bias)
```

```python
import jax
import jax.numpy as jnp
from jax import lax
from jax.experimental import pallas as pl
from jax.experimental.pallas import tpu as pltpu
from jax.sharding import PartitionSpec as P

F32 = jnp.float32
BF16 = jnp.bfloat16
LOG2E = 1.4426950408889634
LN2 = 0.6931471805599453
T = 128
E = 2048
N = 16
RANK = 64
KT = E // 128
S = 8
L = T // S
COLS = RANK + 2 * N
ROWS = 192
HALF = ROWS // 2
MESH = pl.DeviceIdType.MESH
VMEM = pl.BlockSpec(memory_space=pltpu.VMEM)
SMEM = pl.BlockSpec(memory_space=pltpu.SMEM)


def lanes(k):
    return pl.ds(pl.multiple_of(k * 128, 128), 128)


def store_permuted(ref, k, value):
    for blk in range(T // 8):
        first = (blk % 2) * 64 + blk // 2
        ref[k, pl.ds(first, 8, stride=8), :] = value[blk * 8 : blk * 8 + 8, :]


def load_natural(ref, k):
    parts = []
    for blk in range(T // 8):
        first = (blk % 2) * 64 + blk // 2
        parts.append(ref[k, pl.ds(first, 8, stride=8), :])
    return jnp.concatenate(parts, axis=0)


def sigmoid(v):
    return 1.0 / (1.0 + jnp.exp(-v))


def softplus(v):
    z = jnp.exp(-jnp.abs(v))
    r = z / (z + 2.0)
    q = r * r
    poly = 1.0 / 15.0
    for odd in (13.0, 11.0, 9.0, 7.0, 5.0, 3.0, 1.0):
        poly = poly * q + 1.0 / odd
    return jnp.maximum(v, 0.0) + 2.0 * r * poly


def live_mask(len_ref):
    t0 = lax.axis_index("seq") * T
    pos = t0 + lax.broadcasted_iota(jnp.int32, (T, 128), 0)
    return (pos < len_ref[0]).astype(F32)


def fid_row(lab_ref, fid_ref, ls):
    label = lab_ref[0]
    row = jnp.zeros((1, 128), F32)
    for kind in range(2):
        row = row + jnp.where(label == kind, fid_ref[kind : kind + 1, ls], 0.0)
    return row


def row8(ref, n, ls):
    return jnp.broadcast_to(ref[n : n + 1, ls], (8, 128))


def phase_one(
    len_ref, lab_ref, u_ref, gate_ref, gg_ref, xp_ref, dtp_ref, dtb_ref, fid_ref, a2_ref,
    step_ref, su_ref, gy_ref, bb_ref, cb_ref, segs_ref, hs_ref, as_ref, send_ref, low_ref, a2w,
):
    proj = jnp.dot(u_ref[0], xp_ref[...], preferred_element_type=F32)
    low_ref[...] = proj[:, :RANK].astype(BF16)
    for n in range(N):
        for col, ref in ((RANK + n, bb_ref), (RANK + N + n, cb_ref)):
            wide = jnp.broadcast_to(proj[:, col : col + 1], (T, 128))
            for blk in range(T // 8):
                first = (blk % 2) * 8 * (N * S) + n * S + blk // 2
                ref[pl.ds(first, 8, stride=N * S), :] = wide[blk * 8 : blk * 8 + 8, :]
    live = live_mask(len_ref)

    @pl.loop(0, KT)
    def _(k):
        ls = lanes(k)
        dt_raw = (
            jnp.dot(low_ref[...], dtp_ref[:, ls], preferred_element_type=F32)
            + dtb_ref[:, ls]
            + fid_row(lab_ref, fid_ref, ls)
        )
        step = softplus(dt_raw) * live
        u = u_ref[0, :, ls].astype(F32)
        gate = gate_ref[0, :, ls].astype(F32)
        gy = gg_ref[0, :, ls].astype(F32) * live * (gate * sigmoid(gate))
        store_permuted(step_ref, k, step)
        store_permuted(su_ref, k, step * u)
        store_permuted(gy_ref, k, gy)
        for n in range(N):
            a2w[k, n * S : n * S + S, :] = row8(a2_ref, n, ls)

    GN, GK = 4, 2

    @pl.loop(0, KT // GK)
    def _(kp):
        @pl.loop(0, N // GN)
        def _(ng):
            ks = [kp * GK + i for i in range(GK)]
            ns = [ng * GN + i for i in range(GN)]
            a2 = [[a2w[k, pl.ds(pl.multiple_of(n * S, S), S), :] for k in ks] for n in ns]
            h = [[None] * GK for _ in ns]
            pr = [[None] * GK for _ in ns]
            acc = [[None] * GK for _ in ns]
            for tau in range(L):
                rows = pl.ds(tau * S, S)
                st = [step_ref[k, rows, :] for k in ks]
                su = [su_ref[k, rows, :] for k in ks]
                gy = [gy_ref[k, rows, :] for k in ks]
                for j, n in enumerate(ns):
                    at = pl.ds(pl.multiple_of(tau * N * S + n * S, S), S)
                    b = bb_ref[at, :]
                    c = cb_ref[at, :]
                    for i in range(GK):
                        d = jnp.exp2(a2[j][i] * st[i])
                        bs = b * su[i]
                        cg = c * gy[i]
                        if tau == 0:
                            h[j][i], pr[j][i] = bs, d
                            acc[j][i] = d * cg
                        else:
                            h[j][i] = d * h[j][i] + bs
                            pr[j][i] = pr[j][i] * d
                            acc[j][i] = acc[j][i] + pr[j][i] * cg
            for j, n in enumerate(ns):
                at = pl.ds(pl.multiple_of(n * S, S), S)
                for i, k in enumerate(ks):
                    hs_ref[k, at, :] = h[j][i]
                    as_ref[k, at, :] = acc[j][i]

    @pl.loop(0, KT)
    def _(k):
        seg = step_ref[k, pl.ds(0, S), :]
        for tau in range(1, L):
            seg = seg + step_ref[k, pl.ds(tau * S, S), :]
        segs_ref[k] = seg
        for nh in range(2):
            a2 = a2_ref[nh * 8 : nh * 8 + 8, lanes(k)]
            ps = [jnp.exp2(a2 * seg[s : s + 1, :]) for s in range(S)]
            h = hs_ref[k, pl.ds(nh * 64, 8, stride=8), :]
            for s in range(1, S):
                h = ps[s] * h + hs_ref[k, pl.ds(nh * 64 + s, 8, stride=8), :]
            g = as_ref[k, pl.ds(nh * 64 + S - 1, 8, stride=8), :]
            for s in range(S - 2, -1, -1):
                g = ps[s] * g + as_ref[k, pl.ds(nh * 64 + s, 8, stride=8), :]
            send_ref[k, pl.ds(nh * 8, 8), :] = h
            send_ref[k, pl.ds(16 + nh * 8, 8), :] = g
        total = jnp.sum(seg, axis=0, keepdims=True)
        send_ref[k, pl.ds(32, 8), :] = jnp.broadcast_to(total, (8, 128))


def exchange(send_ref, a2_ref, out_ref, got, back, ssem, rsem, ssem2, rsem2):
    size = lax.axis_size("seq")
    me = lax.axis_index("seq")
    barrier = pltpu.get_barrier_semaphore()
    for o in range(1, size):
        j = lax.rem(me + o, size)
        pl.semaphore_signal(barrier, inc=1, device_id={"seq": j}, device_id_type=MESH)
    pl.semaphore_wait(barrier, size - 1)

    def there(j, slot):
        return pltpu.make_async_remote_copy(
            src_ref=send_ref.at[j], dst_ref=got.at[slot], send_sem=ssem.at[j],
            recv_sem=rsem.at[slot], device_id={"seq": j}, device_id_type=MESH,
        )

    def home(j, slot):
        return pltpu.make_async_remote_copy(
            src_ref=back.at[j], dst_ref=out_ref.at[slot], send_sem=ssem2.at[j],
            recv_sem=rsem2.at[slot], device_id={"seq": j}, device_id_type=MESH,
        )

    for o in range(1, size):
        there(lax.rem(me + o, size), me).start()
    got[pl.ds(me, 1)] = send_ref[pl.ds(me, 1)]
    a2 = a2_ref[:, pl.ds(pl.multiple_of(me * 128, 128), 128)]
    for o in range(1, size):
        j = lax.rem(me + o, size)
        there(j, j).wait_recv()
    h = jnp.zeros((N, 128), F32)
    for i in range(size):
        back[i, 0:16, :] = h
        h = jnp.exp2(a2 * got[i, 32:33, :]) * h + got[i, 0:16, :]
    g = jnp.zeros((N, 128), F32)
    for i in range(size - 1, -1, -1):
        back[i, 16:32, :] = g
        g = jnp.exp2(a2 * got[i, 32:33, :]) * g + got[i, 16:32, :]
    for o in range(1, size):
        home(lax.rem(me + o, size), me).start()
    out_ref[pl.ds(me, 1)] = back[pl.ds(me, 1)]
    for o in range(1, size):
        j = lax.rem(me + o, size)
        home(j, j).wait_recv()
    for o in range(1, size):
        j = lax.rem(me + o, size)
        there(j, me).wait_send()
        home(j, me).wait_send()


def phase_two(
    len_ref, lab_ref, u_ref, gate_ref, gg_ref, xp_ref, dtp_ref, dtb_ref, fid_ref, a2_ref,
    skip_ref, step_ref, su_ref, gy_ref, bb_ref, cb_ref, segs_ref, hs_ref, as_ref, st_ref, low_ref,
    gated_ref, gin_ref, ggate_ref, grads_ref,
    hst, gst, hbuf, bgr, cgr, ybuf, sbuf, gbuf, agbuf, dtg, dirs,
):
    @pl.loop(0, KT)
    def _(k):
        for nh in range(2):
            a2 = a2_ref[nh * 8 : nh * 8 + 8, lanes(k)]
            ps = [jnp.exp2(a2 * segs_ref[k, s : s + 1, :]) for s in range(S)]
            h = st_ref[k, nh * 8 : nh * 8 + 8, :]
            for s in range(S):
                at = pl.ds(nh * 64 + s, 8, stride=8)
                hst[k, at, :] = h
                if s + 1 < S:
                    h = ps[s] * h + hs_ref[k, at, :]
            g = st_ref[k, 16 + nh * 8 : 24 + nh * 8, :]
            for s in range(S - 1, -1, -1):
                at = pl.ds(nh * 64 + s, 8, stride=8)
                gst[k, at, :] = g
                if s > 0:
                    g = ps[s] * g + as_ref[k, at, :]

    bgr[...] = jnp.zeros_like(bgr)
    cgr[...] = jnp.zeros_like(cgr)
    GK = 2

    @pl.loop(0, KT // GK)
    def _(kp):
        ks = [kp * GK + i for i in range(GK)]
        FN = 8
        for ng in range(N // FN):
            ns = [ng * FN + j for j in range(FN)]
            a2 = [[row8(a2_ref, n, lanes(k)) for k in ks] for n in ns]
            first = []
            for n in ns:
                for i, k in enumerate(ks):
                    h = hst[k, n * S : n * S + S, :]
                    hbuf[n * GK + i] = h
                    first.append(h)

            def ahead(tau, hh):
                rows = pl.ds(pl.multiple_of(tau * S, S), S)
                st = [step_ref[k, rows, :] for k in ks]
                su = [su_ref[k, rows, :] for k in ks]
                gy = [gy_ref[k, rows, :] for k in ks]
                ys = [None] * GK
                out = []
                for j, n in enumerate(ns):
                    at = pl.ds(pl.multiple_of(tau * (N * S) + n * S, S), S)
                    b = bb_ref[at, :]
                    c = cb_ref[at, :]
                    cg = None
                    for i in range(GK):
                        d = jnp.exp2(a2[j][i] * st[i])
                        h = d * hh[j * GK + i] + b * su[i]
                        out.append(h)
                        hbuf[(tau + 1) * (N * GK) + n * GK + i] = h
                        part = c * h
                        ys[i] = part if ys[i] is None else ys[i] + part
                        part = h * gy[i]
                        cg = part if cg is None else cg + part
                    cgr[at, :] = cgr[at, :] + cg
                for i, k in enumerate(ks):
                    if ng == 0:
                        ybuf[k, rows, :] = ys[i]
                    else:
                        ybuf[k, rows, :] = ybuf[k, rows, :] + ys[i]
                return tuple(out)

            lax.fori_loop(0, L, ahead, tuple(first))

        BN = 4
        for ng in range(N // BN):
            ns = [ng * BN + j for j in range(BN)]
            a2 = [[row8(a2_ref, n, lanes(k)) for k in ks] for n in ns]
            carry = []
            for n in ns:
                for k in ks:
                    carry.append(gst[k, n * S : n * S + S, :])
            zero = jnp.zeros((S, 128), F32)

            def behind(turn, state):
                tau = L - 1 - turn
                cs, ags = state
                rows = pl.ds(pl.multiple_of(tau * S, S), S)
                st = [step_ref[k, rows, :] for k in ks]
                su = [su_ref[k, rows, :] for k in ks]
                gy = [gy_ref[k, rows, :] for k in ks]
                sb = [None] * GK
                sg = [None] * GK
                new_c, new_a = [], []
                for j, n in enumerate(ns):
                    at = pl.ds(pl.multiple_of(tau * (N * S) + n * S, S), S)
                    b = bb_ref[at, :]
                    c = cb_ref[at, :]
                    bg = None
                    for i in range(GK):
                        d = jnp.exp2(a2[j][i] * st[i])
                        g = c * gy[i] + cs[j * GK + i]
                        part = g * b
                        sb[i] = part if sb[i] is None else sb[i] + part
                        part = g * su[i]
                        bg = part if bg is None else bg + part
                        dg = d * g
                        w = dg * hbuf[tau * (N * GK) + n * GK + i]
                        part = a2[j][i] * w
                        sg[i] = part if sg[i] is None else sg[i] + part
                        new_c.append(dg)
                        new_a.append(ags[j * GK + i] + st[i] * w)
                    bgr[at, :] = bgr[at, :] + bg
                for i, k in enumerate(ks):
                    if ng == 0:
                        sbuf[k, rows, :] = sb[i]
                        gbuf[k, rows, :] = sg[i]
                    else:
                        sbuf[k, rows, :] = sbuf[k, rows, :] + sb[i]
                        gbuf[k, rows, :] = gbuf[k, rows, :] + sg[i]
                return tuple(new_c), tuple(new_a)

            _, ags = lax.fori_loop(0, L, behind, (tuple(carry), (zero,) * (BN * GK)))
            for j, n in enumerate(ns):
                for i, k in enumerate(ks):
                    agbuf[k, n * S : n * S + S, :] = ags[j * GK + i]

    live = live_mask(len_ref)
    label = lab_ref[0]

    @pl.loop(0, KT)
    def _(k):
        ls = lanes(k)
        u = u_ref[0, :, ls].astype(F32)
        gate = gate_ref[0, :, ls].astype(F32)
        sig = sigmoid(gate)
        silu = gate * sig
        og = gg_ref[0, :, ls].astype(F32) * live
        y = load_natural(ybuf, k) + skip_ref[:, ls] * u
        gated_ref[0, :, ls] = (y * silu * live).astype(BF16)
        ggate_ref[0, :, ls] = (og * y * (sig * (1.0 + gate * (1.0 - sig)))).astype(BF16)
        dt_raw = (
            jnp.dot(low_ref[...], dtp_ref[:, ls], preferred_element_type=F32)
            + dtb_ref[:, ls]
            + fid_row(lab_ref, fid_ref, ls)
        )
        step_grad = LN2 * load_natural(gbuf, k) + u * load_natural(sbuf, k)
        dt_grad = step_grad * live * sigmoid(dt_raw)
        dt_b = dt_grad.astype(BF16)
        dtg[:, ls] = dt_b
        grads_ref[k, COLS : COLS + RANK, :] = lax.dot_general(
            low_ref[...], dt_b, (((0,), (0,)), ((), ())), preferred_element_type=F32
        )
        base = COLS + RANK
        for nh in range(2):
            ag = agbuf[k, pl.ds(nh * 64, 8, stride=8), :]
            for s in range(1, S):
                ag = ag + agbuf[k, pl.ds(nh * 64 + s, 8, stride=8), :]
            grads_ref[k, base + nh * 8 : base + nh * 8 + 8, :] = (
                ag * a2_ref[nh * 8 : nh * 8 + 8, ls] * LN2
            )
        skip_row = jnp.sum(og * silu * u, axis=0, keepdims=True)
        dt_row = jnp.sum(dt_grad, axis=0, keepdims=True)
        zero = jnp.zeros_like(dt_row)
        grads_ref[k, base + 16 : base + 24, :] = jnp.concatenate(
            [
                skip_row,
                dt_row,
                jnp.where(label == 0, dt_row, zero),
                jnp.where(label == 1, dt_row, zero),
                zero, zero, zero, zero,
            ],
            axis=0,
        )
        grads_ref[k, base + 24 : ROWS, :] = jnp.zeros((ROWS - base - 24, 128), F32)

    low_grad = lax.dot_general(
        dtg[...], dtp_ref[...], (((1,), (1,)), ((), ())), preferred_element_type=F32
    )
    lane = lax.broadcasted_iota(jnp.int32, (128, 128), 1)
    sums = jnp.zeros((T, 128), F32)
    for n in range(N):
        for col, ref in ((RANK + n, bgr), (RANK + N + n, cgr)):
            tile = jnp.concatenate([ref[tau * N * S + n * S : tau * N * S + n * S + S, :] for tau in range(L)], axis=0)
            hi = tile.astype(BF16)
            lo = (tile - hi.astype(F32)).astype(BF16)
            pick = (lane == col).astype(BF16)
            sums = sums + jnp.dot(hi, pick, preferred_element_type=F32)
            sums = sums + jnp.dot(lo, pick, preferred_element_type=F32)
    dirs[0] = sums
    sums = load_natural(dirs, 0)
    proj_grad = jnp.concatenate([low_grad, sums[:, RANK:COLS]], axis=1).astype(BF16)

    @pl.loop(0, KT)
    def _(k):
        ls = lanes(k)
        grads_ref[k, 0:COLS, :] = lax.dot_general(
            proj_grad, u_ref[0, :, ls], (((0,), (0,)), ((), ())), preferred_element_type=F32
        )
        back = lax.dot_general(
            proj_grad, xp_ref[ls, :], (((1,), (1,)), ((), ())), preferred_element_type=F32
        )
        direct = load_natural(step_ref, k) * load_natural(sbuf, k)
        gin_ref[0, :, ls] = (direct + load_natural(gy_ref, k) * skip_ref[:, ls] + back).astype(BF16)


def reduce_grads(g_ref, out_ref, pair, part, peers, mine, zparts, zsum, sems_a, sems_b, sems_c, sems_d):
    chips = lax.axis_size("dp")
    size = lax.axis_size("seq")
    depth = size // 2
    reducers = 6
    rows = HALF // reducers
    dp = lax.axis_index("dp")
    me = lax.axis_index("seq")
    z = me // 2
    core = lax.rem(me, 2)
    sib = me + 1 - 2 * core
    barrier = pltpu.get_barrier_semaphore()
    for o in range(1, chips):
        d = lax.rem(dp + o, chips)
        pl.semaphore_signal(barrier, inc=1, device_id={"dp": d}, device_id_type=MESH)
    for o in range(1, size):
        j = lax.rem(me + o, size)
        pl.semaphore_signal(barrier, inc=1, device_id={"seq": j}, device_id_type=MESH)
    pl.semaphore_wait(barrier, chips + size - 2)

    def to_sib(d):
        return pltpu.make_async_remote_copy(
            src_ref=g_ref.at[d, pl.ds(pl.multiple_of((1 - core) * HALF, 8), HALF)],
            dst_ref=pair.at[d], send_sem=sems_a.at[0, d], recv_sem=sems_a.at[1, d],
            device_id={"seq": sib}, device_id_type=MESH,
        )

    def to_chip(d, slot):
        return pltpu.make_async_remote_copy(
            src_ref=part.at[d], dst_ref=peers.at[slot], send_sem=sems_b.at[0, d],
            recv_sem=sems_b.at[1, slot], device_id={"dp": d}, device_id_type=MESH,
        )

    def to_level(r, slot):
        return pltpu.make_async_remote_copy(
            src_ref=mine.at[pl.ds(pl.multiple_of(r * rows, 8), rows)], dst_ref=zparts.at[slot],
            send_sem=sems_c.at[0, r], recv_sem=sems_c.at[1, slot],
            device_id={"seq": r * 2 + core}, device_id_type=MESH,
        )

    def to_all(j, c, r):
        return pltpu.make_async_remote_copy(
            src_ref=zsum,
            dst_ref=out_ref.at[pl.ds(pl.multiple_of(c * HALF + r * rows, 8), rows)],
            send_sem=sems_d.at[0, j], recv_sem=sems_d.at[1, c * reducers + r],
            device_id={"seq": j}, device_id_type=MESH,
        )

    for o in range(chips):
        to_sib(lax.rem(dp + 1 + o, chips)).start()
    own = pl.ds(pl.multiple_of(core * HALF, 8), HALF)
    for o in range(chips):
        d = lax.rem(dp + 1 + o, chips)
        to_sib(d).wait_recv()
        part[pl.ds(d, 1)] = g_ref[pl.ds(d, 1), own] + pair[pl.ds(d, 1)]
        if o < chips - 1:
            to_chip(d, dp).start()
    total = part[dp]
    for o in range(1, chips):
        d = lax.rem(dp + chips - o, chips)
        to_chip(d, d).wait_recv()
        total = total + peers[d]
    mine[...] = total
    for r in range(reducers):
        @pl.when(r != z)
        def _():
            to_level(r, z).start()

    @pl.when(z < reducers)
    def _():
        acc = mine[pl.ds(pl.multiple_of(z * rows, 8), rows)]
        for o in range(1, depth):
            q = lax.rem(z + o, depth)
            to_level(z, q).wait_recv()
            acc = acc + zparts[q]
        zsum[...] = acc
        out_ref[pl.ds(pl.multiple_of(core * HALF + z * rows, 8), rows)] = acc
        for o in range(1, size):
            to_all(lax.rem(me + o, size), core, z).start()

    for c in range(2):
        for r in range(reducers):
            @pl.when(jnp.logical_or(c != core, r != z))
            def _():
                to_all(me, c, r).wait_recv()

    for o in range(chips):
        to_sib(lax.rem(dp + 1 + o, chips)).wait_send()
    for o in range(1, chips):
        to_chip(lax.rem(dp + o, chips), dp).wait_send()
    for r in range(reducers):
        @pl.when(r != z)
        def _():
            to_level(r, z).wait_send()

    @pl.when(z < reducers)
    def _():
        for o in range(1, size):
            to_all(lax.rem(me + o, size), core, z).wait_send()


def sds(shape, dtype=F32):
    return jax.ShapeDtypeStruct(shape, dtype)


def call_one(rec_lengths, fid_labels, u, gate, gg, x_proj, dt_proj, dt_bias, fid_bias, a2):
    return pl.pallas_call(
        phase_one,
        out_shape=(
            sds((KT, T, 128)), sds((KT, T, 128)), sds((KT, T, 128)),
            sds((L * N * S, 128)), sds((L * N * S, 128)), sds((KT, S, 128)),
            sds((KT, N * S, 128)), sds((KT, N * S, 128)), sds((KT, 40, 128)), sds((T, RANK), BF16),
        ),
        in_specs=[SMEM, SMEM] + [VMEM] * 8,
        out_specs=(VMEM,) * 10,
        scratch_shapes=[pltpu.VMEM((KT, N * S, 128), F32)],
        compiler_params=pltpu.CompilerParams(vmem_limit_bytes=40 << 20),
        name="phase_one",
    )(rec_lengths, fid_labels, u, gate, gg, x_proj, dt_proj, dt_bias, fid_bias, a2)


def call_exchange(send, a2):
    return pl.pallas_call(
        exchange,
        out_shape=sds((KT, 32, 128)),
        in_specs=[VMEM, VMEM],
        out_specs=VMEM,
        scratch_shapes=[
            pltpu.VMEM((16, 40, 128), F32), pltpu.VMEM((16, 32, 128), F32),
            pltpu.SemaphoreType.DMA((16,)), pltpu.SemaphoreType.DMA((16,)),
            pltpu.SemaphoreType.DMA((16,)), pltpu.SemaphoreType.DMA((16,)),
        ],
        compiler_params=pltpu.CompilerParams(collective_id=0, has_side_effects=True),
        name="exchange",
    )(send, a2)


def call_two(*operands):
    return pl.pallas_call(
        phase_two,
        out_shape=(
            sds((1, T, E), BF16), sds((1, T, E), BF16), sds((1, T, E), BF16), sds((KT, ROWS, 128)),
        ),
        in_specs=[SMEM, SMEM] + [VMEM] * 19,
        out_specs=(VMEM,) * 4,
        scratch_shapes=[
            pltpu.VMEM((KT, N * S, 128), F32), pltpu.VMEM((KT, N * S, 128), F32),
            pltpu.VMEM(((L + 1) * N * 2, S, 128), F32),
            pltpu.VMEM((L * N * S, 128), F32), pltpu.VMEM((L * N * S, 128), F32),
            pltpu.VMEM((KT, T, 128), F32), pltpu.VMEM((KT, T, 128), F32), pltpu.VMEM((KT, T, 128), F32),
            pltpu.VMEM((KT, N * S, 128), F32), pltpu.VMEM((T, E), BF16), pltpu.VMEM((1, T, 128), F32),
        ],
        compiler_params=pltpu.CompilerParams(vmem_limit_bytes=56 << 20),
        name="phase_two",
    )(*operands)


def call_reduce(grads):
    return pl.pallas_call(
        reduce_grads,
        out_shape=sds((ROWS, 128)),
        in_specs=[VMEM],
        out_specs=VMEM,
        scratch_shapes=[
            pltpu.VMEM((16, HALF, 128), F32), pltpu.VMEM((16, HALF, 128), F32),
            pltpu.VMEM((16, HALF, 128), F32), pltpu.VMEM((HALF, 128), F32),
            pltpu.VMEM((8, HALF // 6, 128), F32), pltpu.VMEM((HALF // 6, 128), F32),
            pltpu.SemaphoreType.DMA((2, 16)), pltpu.SemaphoreType.DMA((2, 16)),
            pltpu.SemaphoreType.DMA((2, 8)), pltpu.SemaphoreType.DMA((2, 16)),
        ],
        compiler_params=pltpu.CompilerParams(collective_id=1, has_side_effects=True),
        name="reduce_grads",
    )(grads)


def per_device(
    ssm_input, gate_input, grad_gated, x_proj, dt_proj, dt_bias, fid_bias, a_log, skip_gain,
    rec_lengths, fid_labels,
):
    a2 = (-LOG2E * jnp.exp(a_log)).T
    dtb = dt_bias[None, :]
    common = (
        rec_lengths, fid_labels, ssm_input, gate_input, grad_gated, x_proj, dt_proj, dtb, fid_bias, a2,
    )
    step, su, gy, bb, cb, segs, hs, acc, send, low = call_one(*common)
    starts = call_exchange(send, a2)
    gated, grad_input, grad_gate, grads = call_two(
        *common, skip_gain[None, :], step, su, gy, bb, cb, segs, hs, acc, starts, low
    )
    total = call_reduce(grads)
    base = COLS + RANK
    return (
        gated,
        grad_input,
        grad_gate,
        total[:COLS].T,
        total[COLS:base],
        total[base : base + N].T,
        total[base + N],
        total[base + N + 1],
        total[base + N + 2 : base + N + 4],
    )


def solution(mesh):
    wide = P("dp", "seq", None)
    in_specs = (wide, wide, wide, P(), P(), P(), P(), P(), P(), P("dp"), P("dp"))
    out_specs = (
        wide, wide, wide, P("dp", None), P(None, "dp"), P("dp", None), P("dp"), P("dp"), P(None, "dp"),
    )
    return jax.shard_map(
        per_device, mesh=mesh, in_specs=in_specs, out_specs=out_specs, check_vma=False
    )
```

```python
import jax
import jax.numpy as jnp
from jax import lax
from jax.experimental import pallas as pl
from jax.experimental.pallas import tpu as pltpu
from jax.sharding import PartitionSpec as P

F32 = jnp.float32
BF16 = jnp.bfloat16
LOG2E = 1.4426950408889634
LN2 = 0.6931471805599453
T = 128
E = 2048
N = 16
RANK = 64
KT = E // 128
S = 8
L = T // S
COLS = RANK + 2 * N
ROWS = 96
HALF = ROWS // 2
MESH = pl.DeviceIdType.MESH
VMEM = pl.BlockSpec(memory_space=pltpu.VMEM)
ANY = pl.BlockSpec(memory_space=pl.ANY)
SMEM = pl.BlockSpec(memory_space=pltpu.SMEM)


def lanes(k):
    return pl.ds(pl.multiple_of(k * 128, 128), 128)


def store_permuted(ref, k, value):
    for blk in range(T // 8):
        first = (blk % 2) * 64 + blk // 2
        ref[k, pl.ds(first, 8, stride=8), :] = value[blk * 8 : blk * 8 + 8, :]


def load_natural(ref, k):
    parts = []
    for blk in range(T // 8):
        first = (blk % 2) * 64 + blk // 2
        parts.append(ref[k, pl.ds(first, 8, stride=8), :])
    return jnp.concatenate(parts, axis=0)


def sigmoid(v):
    return 1.0 / (1.0 + jnp.exp(-v))


def softplus(v):
    z = jnp.exp(-jnp.abs(v))
    r = z / (z + 2.0)
    q = r * r
    poly = 1.0 / 15.0
    for odd in (13.0, 11.0, 9.0, 7.0, 5.0, 3.0, 1.0):
        poly = poly * q + 1.0 / odd
    return jnp.maximum(v, 0.0) + 2.0 * r * poly


def live_mask(len_ref):
    t0 = lax.axis_index("seq") * T
    pos = t0 + lax.broadcasted_iota(jnp.int32, (T, 128), 0)
    return (pos < len_ref[0]).astype(F32)


def fid_row(lab_ref, fid_ref, ls):
    label = lab_ref[0]
    row = jnp.zeros((1, 128), F32)
    for kind in range(2):
        row = row + jnp.where(label == kind, fid_ref[kind : kind + 1, ls], 0.0)
    return row


def row8(ref, n, ls):
    return jnp.broadcast_to(ref[n : n + 1, ls], (8, 128))


def tile8(n):
    return pl.ds(pl.multiple_of(n * S, S), S)


def step_kernel(
    len_ref, lab_ref, u_hbm, gate_hbm, gg_hbm, xp_hbm, dtp_hbm, dtb_hbm, fid_hbm, al_hbm, skip_hbm,
    gated_hbm, gin_hbm, ggate_hbm, tot_ref,
    u_ref, gate_ref, gg_ref, xp_ref, dtp_ref, dtb_ref, fid_ref, al_ref, skip_ref, a2_ref, a2w,
    low_ref, step_ref, su_ref, gy_ref, bb_ref, cb_ref, segs_ref, hs_ref, as_ref,
    send_h, send_a, got_h, got_a, back_h, back_a, st_h, st_a,
    hbuf, bgr, cgr, ybuf, sbuf, gbuf, agbuf, dtg, dirs, sl_ref, zg_ref, ds_ref,
    gated_ref, gin_ref, ggate_ref, grads, pair, part, peers, mine, zparts,
    in_sems, out_sems, x_send, x_recv, pair_send, pair_recv, chip_send, chip_recv,
    z_send, z_recv, fin_send, fin_recv,
):
    chips = lax.axis_size("dp")
    size = lax.axis_size("seq")
    depth = size // 2
    dp = lax.axis_index("dp")
    me = lax.axis_index("seq")
    z = me // 2
    core = lax.rem(me, 2)
    sib = me + 1 - 2 * core

    loads = []
    pairs = (
        (u_hbm.at[0], u_ref), (xp_hbm, xp_ref), (dtp_hbm, dtp_ref), (dtb_hbm, dtb_ref), (fid_hbm, fid_ref),
        (gate_hbm.at[0], gate_ref), (gg_hbm.at[0], gg_ref), (al_hbm, al_ref), (skip_hbm, skip_ref),
    )
    for i, (src, dst) in enumerate(pairs):
        copy = pltpu.make_async_copy(src, dst, in_sems.at[i])
        copy.start()
        loads.append(copy)

    barrier = pltpu.get_barrier_semaphore()
    for o in range(1, chips):
        d = lax.rem(dp + o, chips)
        pl.semaphore_signal(barrier, inc=1, device_id={"dp": d}, device_id_type=MESH)
    for o in range(1, size):
        j = lax.rem(me + o, size)
        pl.semaphore_signal(barrier, inc=1, device_id={"seq": j}, device_id_type=MESH)

    def remote(src, dst, send, recv, where):
        return pltpu.make_async_remote_copy(
            src_ref=src, dst_ref=dst, send_sem=send, recv_sem=recv, device_id=where, device_id_type=MESH
        )

    def hop(which, src, dst, j, slot):
        return remote(src.at[j], dst.at[slot], x_send.at[which, j], x_recv.at[which, slot], {"seq": j})

    def there_h(j, slot):
        return hop(0, send_h, got_h, j, slot)

    def there_a(j, slot):
        return hop(1, send_a, got_a, j, slot)

    def home_h(j, slot):
        return hop(2, back_h, st_h, j, slot)

    def home_a(j, slot):
        return hop(3, back_a, st_a, j, slot)

    def to_sib(p, d):
        return remote(
            grads.at[p, d, pl.ds(pl.multiple_of((1 - core) * HALF, 8), HALF)], pair.at[p, d],
            pair_send.at[p, d], pair_recv.at[p, d], {"seq": sib},
        )

    def to_chip(p, d, slot):
        return remote(
            part.at[p, d], peers.at[p, slot], chip_send.at[p, d], chip_recv.at[p, slot], {"dp": d}
        )

    def to_level(p, q, slot):
        return remote(
            mine.at[p], zparts.at[p, slot], z_send.at[p, q], z_recv.at[p, slot], {"seq": q * 2 + core}
        )

    def to_final(p):
        return remote(
            tot_ref.at[p, pl.ds(pl.multiple_of(core * HALF, 8), HALF)],
            tot_ref.at[p, pl.ds(pl.multiple_of(core * HALF, 8), HALF)],
            fin_send.at[p], fin_recv.at[p], {"seq": sib},
        )

    def from_final(p):
        return remote(
            tot_ref.at[p, pl.ds(pl.multiple_of((1 - core) * HALF, 8), HALF)],
            tot_ref.at[p, pl.ds(pl.multiple_of((1 - core) * HALF, 8), HALF)],
            fin_send.at[p], fin_recv.at[p], {"seq": sib},
        )

    loads[0].wait()
    loads[1].wait()
    proj = lax.dot_general(
        u_ref[...], xp_ref[...], (((1,), (1,)), ((), ())), preferred_element_type=F32
    )
    low_ref[...] = proj[:, :RANK].astype(BF16)
    for n in range(N):
        for col, ref in ((RANK + n, bb_ref), (RANK + N + n, cb_ref)):
            wide = jnp.broadcast_to(proj[:, col : col + 1], (T, 128))
            for blk in range(T // 8):
                first = (blk % 2) * 8 * (N * S) + n * S + blk // 2
                ref[pl.ds(first, 8, stride=N * S), :] = wide[blk * 8 : blk * 8 + 8, :]
    for copy in loads[2:]:
        copy.wait()
    a2_ref[...] = -LOG2E * jnp.exp(al_ref[...])
    live = live_mask(len_ref)

    @pl.loop(0, KT)
    def _(k):
        ls = lanes(k)
        dt_raw = (
            jnp.dot(low_ref[...], dtp_ref[:, ls], preferred_element_type=F32)
            + dtb_ref[:, ls]
            + fid_row(lab_ref, fid_ref, ls)
        )
        step = softplus(dt_raw) * live
        u = u_ref[:, ls].astype(F32)
        store_permuted(step_ref, k, step)
        store_permuted(su_ref, k, step * u)
        for n in range(N):
            a2w[k, n * S : n * S + S, :] = row8(a2_ref, n, ls)

    GK = 2

    @pl.loop(0, KT // GK)
    def _(kp):
        ks = [kp * GK + i for i in range(GK)]
        GN = 8

        @pl.loop(0, N // GN)
        def _(ng):
            ns = [ng * GN + j for j in range(GN)]
            a2 = [[a2w[k, tile8(n), :] for k in ks] for n in ns]

            def ahead(tau, hh):
                rows = tile8(tau)
                st = [step_ref[k, rows, :] for k in ks]
                su = [su_ref[k, rows, :] for k in ks]
                out = []
                for j, n in enumerate(ns):
                    b = bb_ref[tile8(tau * N + n), :]
                    for i in range(GK):
                        out.append(jnp.exp2(a2[j][i] * st[i]) * hh[j * GK + i] + b * su[i])
                return tuple(out)

            zero = jnp.zeros((S, 128), F32)
            ends = lax.fori_loop(0, L, ahead, (zero,) * (GN * GK), unroll=16)
            for j, n in enumerate(ns):
                for i, k in enumerate(ks):
                    hs_ref[k, tile8(n), :] = ends[j * GK + i]

    @pl.loop(0, KT)
    def _(k):
        seg = step_ref[k, pl.ds(0, S), :]
        for tau in range(1, L):
            seg = seg + step_ref[k, pl.ds(tau * S, S), :]
        segs_ref[k] = seg
        for nh in range(2):
            a2 = a2_ref[nh * 8 : nh * 8 + 8, lanes(k)]
            h = hs_ref[k, pl.ds(nh * 64, 8, stride=8), :]
            for s in range(1, S):
                h = jnp.exp2(a2 * seg[s : s + 1, :]) * h + hs_ref[k, pl.ds(nh * 64 + s, 8, stride=8), :]
            send_h[k, pl.ds(nh * 8, 8), :] = h
        total = jnp.sum(seg, axis=0, keepdims=True)
        send_h[k, pl.ds(16, 8), :] = jnp.broadcast_to(total, (8, 128))

    pl.semaphore_wait(barrier, chips + size - 2)
    for o in range(1, size):
        there_h(lax.rem(me + o, size), me).start()
    got_h[pl.ds(me, 1)] = send_h[pl.ds(me, 1)]

    @pl.loop(0, KT)
    def _(k):
        ls = lanes(k)
        gate = gate_ref[:, ls].astype(F32)
        sig = sigmoid(gate)
        silu = gate * sig * live
        gg = gg_ref[:, ls].astype(F32)
        sl_ref[:, ls] = silu
        zg_ref[:, ls] = gg * live * (sig * (1.0 + gate * (1.0 - sig)))
        store_permuted(gy_ref, k, gg * silu)

    @pl.loop(0, KT // GK)
    def _(kp):
        ks = [kp * GK + i for i in range(GK)]
        GN = 4

        @pl.loop(0, N // GN)
        def _(ng):
            ns = [ng * GN + j for j in range(GN)]
            a2 = [[a2w[k, tile8(n), :] for k in ks] for n in ns]

            def pull(tau, state):
                rows = tile8(tau)
                cum = [state[i] + step_ref[k, rows, :] for i, k in enumerate(ks)]
                gy = [gy_ref[k, rows, :] for k in ks]
                out = list(cum)
                for j, n in enumerate(ns):
                    c = cb_ref[tile8(tau * N + n), :]
                    for i in range(GK):
                        acc = state[GK + j * GK + i]
                        out.append(acc + jnp.exp2(a2[j][i] * cum[i]) * (c * gy[i]))
                return tuple(out)

            zero = jnp.zeros((S, 128), F32)
            ends = lax.fori_loop(0, L, pull, (zero,) * (GK + GN * GK), unroll=16)
            for j, n in enumerate(ns):
                for i, k in enumerate(ks):
                    as_ref[k, tile8(n), :] = ends[GK + j * GK + i]

    @pl.loop(0, KT)
    def _(k):
        for nh in range(2):
            a2 = a2_ref[nh * 8 : nh * 8 + 8, lanes(k)]
            g = as_ref[k, pl.ds(nh * 64 + S - 1, 8, stride=8), :]
            for s in range(S - 2, -1, -1):
                p = jnp.exp2(a2 * segs_ref[k, s : s + 1, :])
                g = p * g + as_ref[k, pl.ds(nh * 64 + s, 8, stride=8), :]
            send_a[k, pl.ds(nh * 8, 8), :] = g

    for o in range(1, size):
        there_a(lax.rem(me + o, size), me).start()
    got_a[pl.ds(me, 1)] = send_a[pl.ds(me, 1)]

    bgr[...] = jnp.zeros_like(bgr)
    cgr[...] = jnp.zeros_like(cgr)

    a2_mine = a2_ref[:, lanes(me)]
    for o in range(1, size):
        j = lax.rem(me + o, size)
        there_h(j, j).wait_recv()
    h = jnp.zeros((N, 128), F32)
    for i in range(size):
        back_h[i] = h
        h = jnp.exp2(a2_mine * got_h[i, 16:17, :]) * h + got_h[i, 0:16, :]
    for o in range(1, size):
        home_h(lax.rem(me + o, size), me).start()
    st_h[pl.ds(me, 1)] = back_h[pl.ds(me, 1)]

    @pl.loop(0, KT)
    def _(k):
        ls = lanes(k)
        dt_raw = (
            jnp.dot(low_ref[...], dtp_ref[:, ls], preferred_element_type=F32)
            + dtb_ref[:, ls]
            + fid_row(lab_ref, fid_ref, ls)
        )
        ds_ref[:, ls] = live * sigmoid(dt_raw)

    for o in range(1, size):
        j = lax.rem(me + o, size)
        there_a(j, j).wait_recv()
    g = jnp.zeros((N, 128), F32)
    for i in range(size - 1, -1, -1):
        back_a[i] = g
        g = jnp.exp2(a2_mine * got_h[i, 16:17, :]) * g + got_a[i]
    for o in range(1, size):
        home_a(lax.rem(me + o, size), me).start()
    st_a[pl.ds(me, 1)] = back_a[pl.ds(me, 1)]

    for o in range(1, size):
        j = lax.rem(me + o, size)
        home_h(j, j).wait_recv()

    @pl.loop(0, KT)
    def _(k):
        for nh in range(2):
            a2 = a2_ref[nh * 8 : nh * 8 + 8, lanes(k)]
            h = st_h[k, nh * 8 : nh * 8 + 8, :]
            for s in range(S):
                at = pl.ds(nh * 64 + s, 8, stride=8)
                end = hs_ref[k, at, :]
                hs_ref[k, at, :] = h
                if s + 1 < S:
                    h = jnp.exp2(a2 * segs_ref[k, s : s + 1, :]) * h + end

    @pl.loop(0, KT // GK)
    def _(kp):
        ks = [kp * GK + i for i in range(GK)]
        FN = 8
        for ng in range(N // FN):
            ns = [ng * FN + j for j in range(FN)]
            a2 = [[a2w[k, n * S : n * S + S, :] for k in ks] for n in ns]
            first = []
            for n in ns:
                for i, k in enumerate(ks):
                    h = hs_ref[k, n * S : n * S + S, :]
                    hbuf[kp * (L + 1) * N * GK + n * GK + i] = h
                    first.append(h)

            def forward(tau, hh):
                rows = tile8(tau)
                st = [step_ref[k, rows, :] for k in ks]
                su = [su_ref[k, rows, :] for k in ks]
                gy = [gy_ref[k, rows, :] for k in ks]
                ys = [None] * GK
                out = []
                for j, n in enumerate(ns):
                    at = tile8(tau * N + n)
                    b = bb_ref[at, :]
                    c = cb_ref[at, :]
                    cg = None
                    for i in range(GK):
                        h = jnp.exp2(a2[j][i] * st[i]) * hh[j * GK + i] + b * su[i]
                        out.append(h)
                        hbuf[(kp * (L + 1) + tau + 1) * (N * GK) + n * GK + i] = h
                        term = c * h
                        ys[i] = term if ys[i] is None else ys[i] + term
                        term = h * gy[i]
                        cg = term if cg is None else cg + term
                    cgr[at, :] = cgr[at, :] + cg
                for i, k in enumerate(ks):
                    if ng == 0:
                        ybuf[k, rows, :] = ys[i]
                    else:
                        ybuf[k, rows, :] = ybuf[k, rows, :] + ys[i]
                return tuple(out)

            lax.fori_loop(0, L, forward, tuple(first), unroll=16)

    for o in range(1, size):
        j = lax.rem(me + o, size)
        home_a(j, j).wait_recv()

    @pl.loop(0, KT)
    def _(k):
        for nh in range(2):
            a2 = a2_ref[nh * 8 : nh * 8 + 8, lanes(k)]
            g = st_a[k, nh * 8 : nh * 8 + 8, :]
            for s in range(S - 1, -1, -1):
                at = pl.ds(nh * 64 + s, 8, stride=8)
                end = as_ref[k, at, :]
                as_ref[k, at, :] = g
                if s > 0:
                    g = jnp.exp2(a2 * segs_ref[k, s : s + 1, :]) * g + end

    @pl.loop(0, KT // GK)
    def _(kp):
        ks = [kp * GK + i for i in range(GK)]
        BN = 4
        for ng in range(N // BN):
            ns = [ng * BN + j for j in range(BN)]
            a2 = [[a2w[k, n * S : n * S + S, :] for k in ks] for n in ns]
            carry = [as_ref[k, n * S : n * S + S, :] for n in ns for k in ks]
            zero = jnp.zeros((S, 128), F32)

            def behind(turn, state):
                tau = L - 1 - turn
                cs, ags = state
                rows = tile8(tau)
                st = [step_ref[k, rows, :] for k in ks]
                su = [su_ref[k, rows, :] for k in ks]
                gy = [gy_ref[k, rows, :] for k in ks]
                sb = [None] * GK
                sg = [None] * GK
                new_c, new_a = [], []
                for j, n in enumerate(ns):
                    at = tile8(tau * N + n)
                    b = bb_ref[at, :]
                    c = cb_ref[at, :]
                    bg = None
                    for i in range(GK):
                        g = c * gy[i] + cs[j * GK + i]
                        term = g * b
                        sb[i] = term if sb[i] is None else sb[i] + term
                        term = g * su[i]
                        bg = term if bg is None else bg + term
                        dg = jnp.exp2(a2[j][i] * st[i]) * g
                        w = dg * hbuf[(kp * (L + 1) + tau) * (N * GK) + n * GK + i]
                        term = a2[j][i] * w
                        sg[i] = term if sg[i] is None else sg[i] + term
                        new_c.append(dg)
                        new_a.append(ags[j * GK + i] + st[i] * w)
                    bgr[at, :] = bgr[at, :] + bg
                for i, k in enumerate(ks):
                    if ng == 0:
                        sbuf[k, rows, :] = sb[i]
                        gbuf[k, rows, :] = sg[i]
                    else:
                        sbuf[k, rows, :] = sbuf[k, rows, :] + sb[i]
                        gbuf[k, rows, :] = gbuf[k, rows, :] + sg[i]
                return tuple(new_c), tuple(new_a)

            _, ags = lax.fori_loop(0, L, behind, (tuple(carry), (zero,) * (BN * GK)), unroll=16)
            for j, n in enumerate(ns):
                for i, k in enumerate(ks):
                    agbuf[k, n * S : n * S + S, :] = ags[j * GK + i]

    label = lab_ref[0]
    own = pl.ds(pl.multiple_of(core * HALF, 8), HALF)

    def pass_on(p, i):
        d = lax.rem(dp + 1 + i, chips)
        to_sib(p, d).wait_recv()
        part[p, pl.ds(d, 1)] = grads[p, pl.ds(d, 1), own] + pair[p, pl.ds(d, 1)]

    @pl.loop(0, KT)
    def _(i):
        k = lax.rem(dp + 1 + i, chips)
        ls = lanes(k)
        u = u_ref[:, ls].astype(F32)
        silu = sl_ref[:, ls]
        y = load_natural(ybuf, k) + skip_ref[:, ls] * u
        gated_ref[:, ls] = (y * silu).astype(BF16)
        ggate_ref[:, ls] = (y * zg_ref[:, ls]).astype(BF16)
        step_grad = LN2 * load_natural(gbuf, k) + u * load_natural(sbuf, k)
        dt_grad = step_grad * ds_ref[:, ls]
        dt_b = dt_grad.astype(BF16)
        dtg[:, ls] = dt_b
        grads[0, k, 0:RANK, :] = lax.dot_general(
            low_ref[...], dt_b, (((0,), (0,)), ((), ())), preferred_element_type=F32
        )
        for nh in range(2):
            ag = agbuf[k, pl.ds(nh * 64, 8, stride=8), :]
            for s in range(1, S):
                ag = ag + agbuf[k, pl.ds(nh * 64 + s, 8, stride=8), :]
            grads[0, k, RANK + nh * 8 : RANK + nh * 8 + 8, :] = (
                ag * a2_ref[nh * 8 : nh * 8 + 8, ls] * LN2
            )
        skip_row = jnp.sum(gg_ref[:, ls].astype(F32) * silu * u, axis=0, keepdims=True)
        dt_row = jnp.sum(dt_grad, axis=0, keepdims=True)
        zero = jnp.zeros_like(dt_row)
        grads[0, k, RANK + N : RANK + N + 8, :] = jnp.concatenate(
            [
                skip_row,
                dt_row,
                jnp.where(label == 0, dt_row, zero),
                jnp.where(label == 1, dt_row, zero),
                zero, zero, zero, zero,
            ],
            axis=0,
        )
        grads[0, k, RANK + N + 8 : ROWS, :] = jnp.zeros((ROWS - RANK - N - 8, 128), F32)
        to_sib(0, k).start()

        @pl.when(i > 0)
        def _():
            pass_on(0, i - 1)
            d = lax.rem(dp + i, chips)
            to_chip(0, d, dp).start()

    pass_on(0, KT - 1)
    out_gated = pltpu.make_async_copy(gated_ref, gated_hbm.at[0], out_sems.at[0])
    out_gated.start()
    out_ggate = pltpu.make_async_copy(ggate_ref, ggate_hbm.at[0], out_sems.at[1])
    out_ggate.start()

    low_grad = lax.dot_general(
        dtg[...], dtp_ref[...], (((1,), (1,)), ((), ())), preferred_element_type=F32
    )
    lane = lax.broadcasted_iota(jnp.int32, (128, 128), 1)
    sums = jnp.zeros((T, 128), F32)
    for n in range(N):
        for col, ref in ((RANK + n, bgr), (RANK + N + n, cgr)):
            tile = jnp.concatenate(
                [ref[(tau * N + n) * S : (tau * N + n) * S + S, :] for tau in range(L)], axis=0
            )
            hi = tile.astype(BF16)
            lo = (tile - hi.astype(F32)).astype(BF16)
            pick = (lane == col).astype(BF16)
            sums = sums + jnp.dot(hi, pick, preferred_element_type=F32)
            sums = sums + jnp.dot(lo, pick, preferred_element_type=F32)
    dirs[0] = sums
    sums = load_natural(dirs, 0)
    proj_grad = jnp.concatenate([low_grad, sums[:, RANK:COLS]], axis=1).astype(BF16)

    @pl.loop(0, KT)
    def _(i):
        k = lax.rem(dp + 1 + i, chips)
        grads[1, k] = lax.dot_general(
            proj_grad, u_ref[:, lanes(k)], (((0,), (0,)), ((), ())), preferred_element_type=F32
        )
        to_sib(1, k).start()

        @pl.when(i > 0)
        def _():
            pass_on(1, i - 1)
            d = lax.rem(dp + i, chips)
            to_chip(1, d, dp).start()

    pass_on(1, KT - 1)

    @pl.loop(0, KT)
    def _(k):
        ls = lanes(k)
        back = jnp.dot(proj_grad, xp_ref[:, ls], preferred_element_type=F32)
        direct = load_natural(step_ref, k) * load_natural(sbuf, k)
        straight = gg_ref[:, ls].astype(F32) * sl_ref[:, ls] * skip_ref[:, ls]
        gin_ref[:, ls] = (direct + straight + back).astype(BF16)

    out_gin = pltpu.make_async_copy(gin_ref, gin_hbm.at[0], out_sems.at[2])
    out_gin.start()

    for p in range(2):
        total = part[p, dp]
        for o in range(1, chips):
            d = lax.rem(dp + chips - o, chips)
            to_chip(p, d, d).wait_recv()
            total = total + peers[p, d]
        mine[p] = total
        for o in range(1, depth):
            to_level(p, lax.rem(z + o, depth), z).start()
    for p in range(2):
        total = mine[p]
        for o in range(1, depth):
            q = lax.rem(z + o, depth)
            to_level(p, q, q).wait_recv()
            total = total + zparts[p, q]
        tot_ref[p, own, :] = total
        to_final(p).start()
    for p in range(2):
        from_final(p).wait_recv()

    for o in range(1, size):
        j = lax.rem(me + o, size)
        there_h(j, me).wait_send()
        there_a(j, me).wait_send()
        home_h(j, me).wait_send()
        home_a(j, me).wait_send()
    for p in range(2):
        to_final(p).wait_send()
        for d in range(chips):
            to_sib(p, d).wait_send()
        for o in range(1, chips):
            to_chip(p, lax.rem(dp + o, chips), dp).wait_send()
        for o in range(1, depth):
            to_level(p, lax.rem(z + o, depth), z).wait_send()
    out_gated.wait()
    out_ggate.wait()
    out_gin.wait()


def finish(
    gated_in, gin_in, ggate_in, tot_ref,
    gated_out, gin_out, ggate_out, gx_ref, gdt_ref, ga_ref, gs_ref, gb_ref, gf_ref,
    hold, in_sems, out_sems,
):
    chunks = 2
    rows = T // chunks
    ins, outs = [], []
    for i, (src, dst) in enumerate(
        ((gated_in, gated_out), (gin_in, gin_out), (ggate_in, ggate_out))
    ):
        for q in range(chunks):
            at = pl.ds(q * rows, rows)
            one = i * chunks + q
            ins.append(pltpu.make_async_copy(src.at[0, at], hold.at[i, at], in_sems.at[one]))
            outs.append(pltpu.make_async_copy(hold.at[i, at], dst.at[0, at], out_sems.at[one]))
    for copy in ins:
        copy.start()
    base = RANK + N
    gx_ref[...] = tot_ref[1]
    gdt_ref[...] = tot_ref[0, 0:RANK, :]
    ga_ref[...] = tot_ref[0, RANK:base, :]
    gs_ref[...] = tot_ref[0, base : base + 1, :]
    gb_ref[...] = tot_ref[0, base + 1 : base + 2, :]
    gf_ref[...] = tot_ref[0, base + 2 : base + 4, :]
    for into, out in zip(ins, outs):
        into.wait()
        out.start()
    for out in outs:
        out.wait()


def sds(shape, dtype=F32):
    return jax.ShapeDtypeStruct(shape, dtype)


def vm(shape, dtype=F32):
    return pltpu.VMEM(shape, dtype)


def call_step(*operands):
    dma = pltpu.SemaphoreType.DMA
    big = sds((1, T, E), BF16)
    return pl.pallas_call(
        step_kernel,
        out_shape=(big, big, big, sds((2, ROWS, 128))),
        in_specs=[SMEM, SMEM] + [ANY] * 9,
        out_specs=(ANY, ANY, ANY, VMEM),
        scratch_shapes=[
            vm((T, E), BF16), vm((T, E), BF16), vm((T, E), BF16), vm((COLS, E), BF16), vm((RANK, E), BF16),
            vm((1, E)), vm((2, E)), vm((N, E)), vm((1, E)), vm((N, E)), vm((KT, N * S, 128)),
            vm((T, RANK), BF16), vm((KT, T, 128)), vm((KT, T, 128)), vm((KT, T, 128)),
            vm((L * N * S, 128)), vm((L * N * S, 128)), vm((KT, S, 128)),
            vm((KT, N * S, 128)), vm((KT, N * S, 128)),
            vm((16, 24, 128)), vm((16, 16, 128)), vm((16, 24, 128)), vm((16, 16, 128)),
            vm((16, 16, 128)), vm((16, 16, 128)), vm((16, 16, 128)), vm((16, 16, 128)),
            vm((KT * (L + 1) * N, S, 128)), vm((L * N * S, 128)), vm((L * N * S, 128)),
            vm((KT, T, 128)), vm((KT, T, 128)), vm((KT, T, 128)), vm((KT, N * S, 128)),
            vm((T, E), BF16), vm((1, T, 128)), vm((T, E)), vm((T, E)), vm((T, E)),
            vm((T, E), BF16), vm((T, E), BF16), vm((T, E), BF16),
            vm((2, 16, ROWS, 128)), vm((2, 16, HALF, 128)), vm((2, 16, HALF, 128)),
            vm((2, 16, HALF, 128)), vm((2, HALF, 128)), vm((2, 8, HALF, 128)),
            dma((9,)), dma((3,)), dma((4, 16)), dma((4, 16)), dma((2, 16)), dma((2, 16)),
            dma((2, 16)), dma((2, 16)), dma((2, 8)), dma((2, 8)), dma((2,)), dma((2,)),
        ],
        compiler_params=pltpu.CompilerParams(
            collective_id=0, has_side_effects=True, vmem_limit_bytes=60 << 20
        ),
        name="step_kernel",
    )(*operands)


def call_finish(*operands):
    big = sds((1, T, E), BF16)
    return pl.pallas_call(
        finish,
        out_shape=(
            big, big, big, sds((COLS, 128)), sds((RANK, 128)), sds((N, 128)), sds((1, 128)),
            sds((1, 128)), sds((2, 128)),
        ),
        in_specs=[ANY, ANY, ANY, VMEM],
        out_specs=(ANY, ANY, ANY) + (VMEM,) * 6,
        scratch_shapes=[
            vm((3, T, E), BF16), pltpu.SemaphoreType.DMA((6,)), pltpu.SemaphoreType.DMA((6,)),
        ],
        name="finish",
    )(*operands)


def per_device(
    ssm_input, gate_input, grad_gated, x_proj, dt_proj, dt_bias, fid_bias, a_log, skip_gain,
    rec_lengths, fid_labels,
):
    results = call_step(
        rec_lengths, fid_labels, ssm_input, gate_input, grad_gated, x_proj.T, dt_proj,
        dt_bias[None, :], fid_bias, a_log.T, skip_gain[None, :],
    )
    gated, gin, ggate, gx, gdt, ga, gs, gb, gf = call_finish(*results)
    return (gated, gin, ggate, gx.T, gdt, ga.T, gs[0], gb[0], gf)


def solution(mesh):
    wide = P("dp", "seq", None)
    in_specs = (wide, wide, wide, P(), P(), P(), P(), P(), P(), P("dp"), P("dp"))
    out_specs = (
        wide, wide, wide, P("dp", None), P(None, "dp"), P("dp", None), P("dp"), P("dp"), P(None, "dp"),
    )
    return jax.shard_map(
        per_device, mesh=mesh, in_specs=in_specs, out_specs=out_specs, check_vma=False
    )
```

```python
import jax
import jax.numpy as jnp
from jax import lax
from jax.experimental import pallas as pl
from jax.experimental.pallas import tpu as pltpu
from jax.sharding import PartitionSpec as P

F32 = jnp.float32
BF16 = jnp.bfloat16
LOG2E = 1.4426950408889634
LN2 = 0.6931471805599453
T = 128
E = 2048
N = 16
RANK = 64
KT = E // 128
S = 8
L = T // S
COLS = RANK + 2 * N
ROWS_D = 128
ROWS_X = 64
HALF_D = ROWS_D // 2
HALF_X = ROWS_X // 2
MESH = pl.DeviceIdType.MESH
VMEM = pl.BlockSpec(memory_space=pltpu.VMEM)
ANY = pl.BlockSpec(memory_space=pl.ANY)
SMEM = pl.BlockSpec(memory_space=pltpu.SMEM)


def lanes(k):
    return pl.ds(pl.multiple_of(k * 128, 128), 128)


def store_permuted(ref, k, value):
    for blk in range(T // 8):
        first = (blk % 2) * 64 + blk // 2
        ref[k, pl.ds(first, 8, stride=8), :] = value[blk * 8 : blk * 8 + 8, :]


def load_natural(ref, k):
    parts = []
    for blk in range(T // 8):
        first = (blk % 2) * 64 + blk // 2
        parts.append(ref[k, pl.ds(first, 8, stride=8), :])
    return jnp.concatenate(parts, axis=0)


def sigmoid(v):
    return 1.0 / (1.0 + jnp.exp(-v))


def softplus(v):
    z = jnp.exp(-jnp.abs(v))
    r = z / (z + 2.0)
    q = r * r
    poly = 1.0 / 15.0
    for odd in (13.0, 11.0, 9.0, 7.0, 5.0, 3.0, 1.0):
        poly = poly * q + 1.0 / odd
    return jnp.maximum(v, 0.0) + 2.0 * r * poly


def live_mask(len_ref):
    t0 = lax.axis_index("seq") * T
    pos = t0 + lax.broadcasted_iota(jnp.int32, (T, 128), 0)
    return (pos < len_ref[0]).astype(F32)


def fid_row(lab_ref, fid_ref, ls):
    label = lab_ref[0]
    row = jnp.zeros((1, 128), F32)
    for kind in range(2):
        row = row + jnp.where(label == kind, fid_ref[kind : kind + 1, ls], 0.0)
    return row


def row8(ref, n, ls):
    return jnp.broadcast_to(ref[n : n + 1, ls], (8, 128))


def tile8(n):
    return pl.ds(pl.multiple_of(n * S, S), S)


def step_kernel(
    len_ref, lab_ref, u_hbm, gate_hbm, gg_hbm, xp_hbm, dtp_hbm, dtb_hbm, fid_hbm, al_hbm, skip_hbm,
    gated_hbm, gin_hbm, ggate_hbm, tot_d, tot_x,
    u_ref, gate_ref, gg_ref, xp_ref, dtp_ref, dtb_ref, fid_ref, al_ref, skip_ref, a2_ref, a2w,
    low_ref, step_ref, su_ref, gy_ref, bb_ref, cb_ref, segs_ref, hs_ref, as_ref,
    send_h, send_a, got_h, got_a, back_h, back_a, st_h, st_a,
    hbuf, bgr, cgr, ybuf, sbuf, gbuf, agbuf, dtg, dirs, sl_ref, zg_ref, ds_ref,
    gated_ref, gin_ref, ggate_ref, bcg_ref,
    grads_d, pair_d, part_d, peers_d, mine_d, zparts_d, grads_x, pair_x, part_x, peers_x, mine_x, zparts_x,
    in_sems, out_sems, x_send, x_recv, pair_send, pair_recv, chip_send, chip_recv,
    z_send, z_recv, fin_send, fin_recv, all_send, all_recv,
):
    chips = lax.axis_size("dp")
    size = lax.axis_size("seq")
    depth = size // 2
    dp = lax.axis_index("dp")
    me = lax.axis_index("seq")
    z = me // 2
    core = lax.rem(me, 2)
    sib = me + 1 - 2 * core

    loads = []
    pairs = (
        (u_hbm.at[0], u_ref), (xp_hbm, xp_ref), (dtp_hbm, dtp_ref), (dtb_hbm, dtb_ref), (fid_hbm, fid_ref),
        (gate_hbm.at[0], gate_ref), (gg_hbm.at[0], gg_ref), (al_hbm, al_ref), (skip_hbm, skip_ref),
    )
    for i, (src, dst) in enumerate(pairs):
        copy = pltpu.make_async_copy(src, dst, in_sems.at[i])
        copy.start()
        loads.append(copy)

    barrier = pltpu.get_barrier_semaphore()
    for o in range(1, chips):
        d = lax.rem(dp + o, chips)
        pl.semaphore_signal(barrier, inc=1, device_id={"dp": d}, device_id_type=MESH)
    for o in range(1, size):
        j = lax.rem(me + o, size)
        pl.semaphore_signal(barrier, inc=1, device_id={"seq": j}, device_id_type=MESH)

    def remote(src, dst, send, recv, where):
        return pltpu.make_async_remote_copy(
            src_ref=src, dst_ref=dst, send_sem=send, recv_sem=recv, device_id=where, device_id_type=MESH
        )

    def hop(which, src, dst, j, slot):
        return remote(src.at[j], dst.at[slot], x_send.at[which, j], x_recv.at[which, slot], {"seq": j})

    def there_h(j, slot):
        return hop(0, send_h, got_h, j, slot)

    def there_a(j, slot):
        return hop(1, send_a, got_a, j, slot)

    def home_h(j, slot):
        return hop(2, back_h, st_h, j, slot)

    def home_a(j, slot):
        return hop(3, back_a, st_a, j, slot)

    def group(g):
        return [2 * lax.rem(z + o, depth) + g for o in range(1, depth)]

    def send_group(copy, g, src, dst):
        for j in group(g):
            copy(j, me).start()

        @pl.when(core != g)
        def _():
            copy(sib, me).start()

        @pl.when(core == g)
        def _():
            dst[pl.ds(me, 1)] = src[pl.ds(me, 1)]

    def wait_group(copy, g):
        for j in group(g):
            copy(j, j).wait_recv()

        @pl.when(core != g)
        def _():
            copy(sib, sib).wait_recv()

    grads, pair, part = (grads_d, grads_x), (pair_d, pair_x), (part_d, part_x)
    peers, mine, zparts = (peers_d, peers_x), (mine_d, mine_x), (zparts_d, zparts_x)
    halves = (HALF_D, HALF_X)

    def half_of(p, c):
        return pl.ds(pl.multiple_of(c * halves[p], 8), halves[p])

    def to_sib(p, d):
        return remote(
            grads[p].at[d, half_of(p, 1 - core)], pair[p].at[d],
            pair_send.at[p, d], pair_recv.at[p, d], {"seq": sib},
        )

    def to_chip(p, d, slot):
        return remote(
            part[p].at[d], peers[p].at[slot], chip_send.at[p, d], chip_recv.at[p, slot], {"dp": d}
        )

    def to_level(p, q, slot):
        src = mine_x if p else mine_d.at[pl.ds(pl.multiple_of(q * 8, 8), 8)]
        return remote(
            src, zparts[p].at[slot], z_send.at[p, q], z_recv.at[p, slot], {"seq": q * 2 + core}
        )

    def gather_d(j, c, q):
        here = tot_d.at[pl.ds(pl.multiple_of(c * HALF_D + q * 8, 8), 8)]
        return remote(here, here, all_send.at[j], all_recv.at[2 * q + c], {"seq": j})

    def last(c):
        here = tot_x.at[half_of(1, c)]
        return remote(here, here, fin_send.at[0], fin_recv.at[0], {"seq": sib})

    loads[0].wait()
    loads[1].wait()
    proj = lax.dot_general(
        u_ref[...], xp_ref[...], (((1,), (1,)), ((), ())), preferred_element_type=F32
    )
    low_ref[...] = proj[:, :RANK].astype(BF16)
    for n in range(N):
        for col, ref in ((RANK + n, bb_ref), (RANK + N + n, cb_ref)):
            wide = jnp.broadcast_to(proj[:, col : col + 1], (T, 128))
            for blk in range(T // 8):
                first = (blk % 2) * 8 * (N * S) + n * S + blk // 2
                ref[pl.ds(first, 8, stride=N * S), :] = wide[blk * 8 : blk * 8 + 8, :]
    for copy in loads[2:]:
        copy.wait()
    a2_ref[...] = -LOG2E * jnp.exp(al_ref[...])
    live = live_mask(len_ref)

    def dt_before(ls):
        return (
            jnp.dot(low_ref[...], dtp_ref[:, ls], preferred_element_type=F32)
            + dtb_ref[:, ls]
            + fid_row(lab_ref, fid_ref, ls)
        )

    @pl.loop(0, KT // 2)
    def _(turn):
        ks = [turn * 2 + q for q in range(2)]
        raws = [dt_before(lanes(k)) for k in ks]
        for k, dt_raw in zip(ks, raws):
            ls = lanes(k)
            step = softplus(dt_raw) * live
            u = u_ref[:, ls].astype(F32)
            store_permuted(step_ref, k, step)
            store_permuted(su_ref, k, step * u)
            for n in range(N):
                a2w[k, n * S : n * S + S, :] = row8(a2_ref, n, ls)

    GK = 2
    PAIRS = KT // GK

    def tiles_of(g, q):
        return [4 * q + g, 4 * q + 2 + g]

    def zero_ends(g):
        @pl.loop(0, PAIRS // 2)
        def _(q):
            ks = tiles_of(g, q)
            GN = 8

            @pl.loop(0, N // GN)
            def _(ng):
                ns = [ng * GN + j for j in range(GN)]
                a2 = [[a2w[k, tile8(n), :] for k in ks] for n in ns]

                def ahead(tau, hh):
                    rows = tile8(tau)
                    st = [step_ref[k, rows, :] for k in ks]
                    su = [su_ref[k, rows, :] for k in ks]
                    out = []
                    for j, n in enumerate(ns):
                        b = bb_ref[tile8(tau * N + n), :]
                        for i in range(GK):
                            out.append(jnp.exp2(a2[j][i] * st[i]) * hh[j * GK + i] + b * su[i])
                    return tuple(out)

                zero = jnp.zeros((S, 128), F32)
                ends = lax.fori_loop(0, L, ahead, (zero,) * (GN * GK), unroll=16)
                for j, n in enumerate(ns):
                    for i, k in enumerate(ks):
                        hs_ref[k, tile8(n), :] = ends[j * GK + i]

        @pl.loop(0, KT // 2)
        def _(q):
            k = 2 * q + g
            seg = step_ref[k, pl.ds(0, S), :]
            for tau in range(1, L):
                seg = seg + step_ref[k, pl.ds(tau * S, S), :]
            segs_ref[k] = seg
            for nh in range(2):
                a2 = a2_ref[nh * 8 : nh * 8 + 8, lanes(k)]
                h = hs_ref[k, pl.ds(nh * 64, 8, stride=8), :]
                for s in range(1, S):
                    h = jnp.exp2(a2 * seg[s : s + 1, :]) * h + hs_ref[k, pl.ds(nh * 64 + s, 8, stride=8), :]
                send_h[k, pl.ds(nh * 8, 8), :] = h
            total = jnp.sum(seg, axis=0, keepdims=True)
            send_h[k, pl.ds(16, 8), :] = jnp.broadcast_to(total, (8, 128))

    zero_ends(0)
    pl.semaphore_wait(barrier, chips + size - 2)
    send_group(there_h, 0, send_h, got_h)
    zero_ends(1)
    send_group(there_h, 1, send_h, got_h)

    @pl.loop(0, KT // 2)
    def _(turn):
        for q in range(2):
            k = turn * 2 + q
            ls = lanes(k)
            gate = gate_ref[:, ls].astype(F32)
            sig = sigmoid(gate)
            silu = gate * sig * live
            gg = gg_ref[:, ls].astype(F32)
            sl_ref[:, ls] = silu
            zg_ref[:, ls] = gg * live * (sig * (1.0 + gate * (1.0 - sig)))
            store_permuted(gy_ref, k, gg * silu)

    def zero_pulls(g):
        @pl.loop(0, PAIRS // 2)
        def _(q):
            ks = tiles_of(g, q)
            GN = 4

            @pl.loop(0, N // GN)
            def _(ng):
                ns = [ng * GN + j for j in range(GN)]
                a2 = [[a2w[k, tile8(n), :] for k in ks] for n in ns]

                def pull(tau, state):
                    rows = tile8(tau)
                    cum = [state[i] + step_ref[k, rows, :] for i, k in enumerate(ks)]
                    gy = [gy_ref[k, rows, :] for k in ks]
                    out = list(cum)
                    for j, n in enumerate(ns):
                        c = cb_ref[tile8(tau * N + n), :]
                        for i in range(GK):
                            acc = state[GK + j * GK + i]
                            out.append(acc + jnp.exp2(a2[j][i] * cum[i]) * (c * gy[i]))
                    return tuple(out)

                zero = jnp.zeros((S, 128), F32)
                ends = lax.fori_loop(0, L, pull, (zero,) * (GK + GN * GK), unroll=16)
                for j, n in enumerate(ns):
                    for i, k in enumerate(ks):
                        as_ref[k, tile8(n), :] = ends[GK + j * GK + i]

        @pl.loop(0, KT // 2)
        def _(q):
            k = 2 * q + g
            for nh in range(2):
                a2 = a2_ref[nh * 8 : nh * 8 + 8, lanes(k)]
                h = as_ref[k, pl.ds(nh * 64 + S - 1, 8, stride=8), :]
                for s in range(S - 2, -1, -1):
                    p = jnp.exp2(a2 * segs_ref[k, s : s + 1, :])
                    h = p * h + as_ref[k, pl.ds(nh * 64 + s, 8, stride=8), :]
                send_a[k, pl.ds(nh * 8, 8), :] = h

    zero_pulls(0)
    send_group(there_a, 0, send_a, got_a)
    zero_pulls(1)
    send_group(there_a, 1, send_a, got_a)

    bgr[...] = jnp.zeros_like(bgr)
    cgr[...] = jnp.zeros_like(cgr)

    a2_mine = a2_ref[:, lanes(me)]
    for o in range(1, size):
        j = lax.rem(me + o, size)
        there_h(j, j).wait_recv()
    h = jnp.zeros((N, 128), F32)
    for i in range(size):
        back_h[i] = h
        h = jnp.exp2(a2_mine * got_h[i, 16:17, :]) * h + got_h[i, 0:16, :]
    for o in range(1, size):
        home_h(lax.rem(me + o, size), me).start()
    st_h[pl.ds(me, 1)] = back_h[pl.ds(me, 1)]

    @pl.loop(0, KT // 4)
    def _(turn):
        ks = [turn * 4 + q for q in range(4)]
        raws = [dt_before(lanes(k)) for k in ks]
        for k, dt_raw in zip(ks, raws):
            ds_ref[:, lanes(k)] = live * sigmoid(dt_raw)

    for o in range(1, size):
        j = lax.rem(me + o, size)
        there_a(j, j).wait_recv()
    g = jnp.zeros((N, 128), F32)
    for i in range(size - 1, -1, -1):
        back_a[i] = g
        g = jnp.exp2(a2_mine * got_h[i, 16:17, :]) * g + got_a[i]
    for o in range(1, size):
        home_a(lax.rem(me + o, size), me).start()
    st_a[pl.ds(me, 1)] = back_a[pl.ds(me, 1)]

    def full_forward(g):
        wait_group(home_h, g)

        @pl.loop(0, KT // 2)
        def _(q):
            k = 2 * q + g
            for nh in range(2):
                a2 = a2_ref[nh * 8 : nh * 8 + 8, lanes(k)]
                h = st_h[k, nh * 8 : nh * 8 + 8, :]
                for s in range(S):
                    at = pl.ds(nh * 64 + s, 8, stride=8)
                    end = hs_ref[k, at, :]
                    hs_ref[k, at, :] = h
                    if s + 1 < S:
                        h = jnp.exp2(a2 * segs_ref[k, s : s + 1, :]) * h + end

        @pl.loop(0, PAIRS // 2)
        def _(q):
            ks = tiles_of(g, q)
            kp = g * (PAIRS // 2) + q
            FN = 8
            for ng in range(N // FN):
                ns = [ng * FN + j for j in range(FN)]
                a2 = [[a2w[k, n * S : n * S + S, :] for k in ks] for n in ns]
                first = []
                for n in ns:
                    for i, k in enumerate(ks):
                        h = hs_ref[k, n * S : n * S + S, :]
                        hbuf[kp * (L + 1) * N * GK + n * GK + i] = h
                        first.append(h)

                def forward(tau, hh):
                    rows = tile8(tau)
                    st = [step_ref[k, rows, :] for k in ks]
                    su = [su_ref[k, rows, :] for k in ks]
                    gy = [gy_ref[k, rows, :] for k in ks]
                    ys = [None] * GK
                    out = []
                    for j, n in enumerate(ns):
                        at = tile8(tau * N + n)
                        b = bb_ref[at, :]
                        c = cb_ref[at, :]
                        cg = None
                        for i in range(GK):
                            h = jnp.exp2(a2[j][i] * st[i]) * hh[j * GK + i] + b * su[i]
                            out.append(h)
                            hbuf[(kp * (L + 1) + tau + 1) * (N * GK) + n * GK + i] = h
                            term = c * h
                            ys[i] = term if ys[i] is None else ys[i] + term
                            term = h * gy[i]
                            cg = term if cg is None else cg + term
                        cgr[at, :] = cgr[at, :] + cg
                    for i, k in enumerate(ks):
                        if ng == 0:
                            ybuf[k, rows, :] = ys[i]
                        else:
                            ybuf[k, rows, :] = ybuf[k, rows, :] + ys[i]
                    return tuple(out)

                lax.fori_loop(0, L, forward, tuple(first), unroll=16)

    full_forward(0)
    full_forward(1)

    def full_backward(g):
        wait_group(home_a, g)

        @pl.loop(0, KT // 2)
        def _(q):
            k = 2 * q + g
            for nh in range(2):
                a2 = a2_ref[nh * 8 : nh * 8 + 8, lanes(k)]
                h = st_a[k, nh * 8 : nh * 8 + 8, :]
                for s in range(S - 1, -1, -1):
                    at = pl.ds(nh * 64 + s, 8, stride=8)
                    end = as_ref[k, at, :]
                    as_ref[k, at, :] = h
                    if s > 0:
                        h = jnp.exp2(a2 * segs_ref[k, s : s + 1, :]) * h + end

        @pl.loop(0, PAIRS // 2)
        def _(q):
            ks = tiles_of(g, q)
            kp = g * (PAIRS // 2) + q
            BN = 4
            for ng in range(N // BN):
                ns = [ng * BN + j for j in range(BN)]
                a2 = [[a2w[k, n * S : n * S + S, :] for k in ks] for n in ns]
                carry = [as_ref[k, n * S : n * S + S, :] for n in ns for k in ks]
                zero = jnp.zeros((S, 128), F32)

                def behind(turn, state):
                    tau = L - 1 - turn
                    cs, ags = state
                    rows = tile8(tau)
                    st = [step_ref[k, rows, :] for k in ks]
                    su = [su_ref[k, rows, :] for k in ks]
                    gy = [gy_ref[k, rows, :] for k in ks]
                    sb = [None] * GK
                    sg = [None] * GK
                    new_c, new_a = [], []
                    for j, n in enumerate(ns):
                        at = tile8(tau * N + n)
                        b = bb_ref[at, :]
                        c = cb_ref[at, :]
                        bg = None
                        for i in range(GK):
                            g = c * gy[i] + cs[j * GK + i]
                            term = g * b
                            sb[i] = term if sb[i] is None else sb[i] + term
                            term = g * su[i]
                            bg = term if bg is None else bg + term
                            dg = jnp.exp2(a2[j][i] * st[i]) * g
                            w = dg * hbuf[(kp * (L + 1) + tau) * (N * GK) + n * GK + i]
                            term = a2[j][i] * w
                            sg[i] = term if sg[i] is None else sg[i] + term
                            new_c.append(dg)
                            new_a.append(ags[j * GK + i] + st[i] * w)
                        bgr[at, :] = bgr[at, :] + bg
                    for i, k in enumerate(ks):
                        if ng == 0:
                            sbuf[k, rows, :] = sb[i]
                            gbuf[k, rows, :] = sg[i]
                        else:
                            sbuf[k, rows, :] = sbuf[k, rows, :] + sb[i]
                            gbuf[k, rows, :] = gbuf[k, rows, :] + sg[i]
                    return tuple(new_c), tuple(new_a)

                _, ags = lax.fori_loop(0, L, behind, (tuple(carry), (zero,) * (BN * GK)), unroll=16)
                for j, n in enumerate(ns):
                    for i, k in enumerate(ks):
                        agbuf[k, n * S : n * S + S, :] = ags[j * GK + i]

    full_backward(0)
    full_backward(1)

    label = lab_ref[0]
    lane = lax.broadcasted_iota(jnp.int32, (128, 128), 1)
    sums = jnp.zeros((T, 128), F32)
    for n in range(N):
        for col, ref in ((n, bgr), (N + n, cgr)):
            tile = jnp.concatenate(
                [ref[(tau * N + n) * S : (tau * N + n) * S + S, :] for tau in range(L)], axis=0
            )
            hi = tile.astype(BF16)
            lo = (tile - hi.astype(F32)).astype(BF16)
            pick = (lane == col).astype(BF16)
            sums = sums + jnp.dot(hi, pick, preferred_element_type=F32)
            sums = sums + jnp.dot(lo, pick, preferred_element_type=F32)
    dirs[0] = sums
    bcg_ref[...] = load_natural(dirs, 0)[:, : 2 * N].astype(BF16)

    def pass_on(p, i):
        d = lax.rem(dp + 1 + i, chips)
        to_sib(p, d).wait_recv()
        part[p][pl.ds(d, 1)] = grads[p][pl.ds(d, 1), half_of(p, core)] + pair[p][pl.ds(d, 1)]

    def send_on(p, i):
        pass_on(p, i)
        to_chip(p, lax.rem(dp + 1 + i, chips), dp).start()

    def early_block(i):
        k = lax.rem(dp + 1 + i, chips)
        ls = lanes(k)
        u = u_ref[:, ls]
        uf = u.astype(F32)
        step_grad = LN2 * load_natural(gbuf, k) + uf * load_natural(sbuf, k)
        dt_grad = step_grad * ds_ref[:, ls]
        dt_b = dt_grad.astype(BF16)
        dtg[:, ls] = dt_b
        grads_d[k, 0:RANK, :] = lax.dot_general(
            low_ref[...], dt_b, (((0,), (0,)), ((), ())), preferred_element_type=F32
        )
        for nh in range(2):
            ag = agbuf[k, pl.ds(nh * 64, 8, stride=8), :]
            for s in range(1, S):
                ag = ag + agbuf[k, pl.ds(nh * 64 + s, 8, stride=8), :]
            grads_d[k, RANK + nh * 8 : RANK + nh * 8 + 8, :] = (
                ag * a2_ref[nh * 8 : nh * 8 + 8, ls] * LN2
            )
        skip_row = jnp.sum(gg_ref[:, ls].astype(F32) * sl_ref[:, ls] * uf, axis=0, keepdims=True)
        dt_row = jnp.sum(dt_grad, axis=0, keepdims=True)
        zero = jnp.zeros_like(dt_row)
        base = RANK + N
        grads_d[k, base : base + 8, :] = jnp.concatenate(
            [
                skip_row,
                dt_row,
                jnp.where(label == 0, dt_row, zero),
                jnp.where(label == 1, dt_row, zero),
                zero, zero, zero, zero,
            ],
            axis=0,
        )
        grads_d[k, base + 8 : base + 8 + 2 * N, :] = lax.dot_general(
            bcg_ref[...], u, (((0,), (0,)), ((), ())), preferred_element_type=F32
        )
        grads_d[k, base + 8 + 2 * N : ROWS_D, :] = jnp.zeros((ROWS_D - base - 8 - 2 * N, 128), F32)
        return k

    def early_turn(turn):
        made = [early_block(turn * 2 + q) for q in range(2)]
        for k in made:
            to_sib(0, k).start()

    early_turn(0)

    @pl.loop(1, KT // 2)
    def _(turn):
        early_turn(turn)
        send_on(0, turn * 2 - 2)
        send_on(0, turn * 2 - 1)

    low_grad = lax.dot_general(
        dtg[...], dtp_ref[...], (((1,), (1,)), ((), ())), preferred_element_type=F32
    ).astype(BF16)
    send_on(0, KT - 2)
    pass_on(0, KT - 1)

    def late_turn(turn):
        made = [lax.rem(dp + 1 + turn * 4 + q, chips) for q in range(4)]
        for k in made:
            grads_x[k] = lax.dot_general(
                low_grad, u_ref[:, lanes(k)], (((0,), (0,)), ((), ())), preferred_element_type=F32
            )
        for k in made:
            to_sib(1, k).start()

    late_turn(0)

    @pl.loop(1, KT // 4)
    def _(turn):
        late_turn(turn)
        for q in range(4):
            send_on(1, turn * 4 - 4 + q)

    for q in range(3):
        send_on(1, KT - 4 + q)
    pass_on(1, KT - 1)

    def add_up(p):
        total = part[p][dp]
        for o in range(1, chips):
            d = lax.rem(dp + chips - o, chips)
            to_chip(p, d, d).wait_recv()
            total = total + peers[p][d]
        mine[p][...] = total
        for o in range(1, depth):
            to_level(p, lax.rem(z + o, depth), z).start()

    @pl.loop(0, KT // 2)
    def _(turn):
        for q in range(2):
            k = turn * 2 + q
            ls = lanes(k)
            y = load_natural(ybuf, k) + skip_ref[:, ls] * u_ref[:, ls].astype(F32)
            gated_ref[:, ls] = (y * sl_ref[:, ls]).astype(BF16)
            ggate_ref[:, ls] = (y * zg_ref[:, ls]).astype(BF16)

    out_gated = pltpu.make_async_copy(gated_ref, gated_hbm.at[0], out_sems.at[0])
    out_gated.start()
    out_ggate = pltpu.make_async_copy(ggate_ref, ggate_hbm.at[0], out_sems.at[1])
    out_ggate.start()
    add_up(0)
    proj_grad = jnp.concatenate([low_grad, bcg_ref[...]], axis=1)

    @pl.loop(0, KT // 2)
    def _(turn):
        for q in range(2):
            k = turn * 2 + q
            ls = lanes(k)
            back = jnp.dot(proj_grad, xp_ref[:, ls], preferred_element_type=F32)
            direct = load_natural(step_ref, k) * load_natural(sbuf, k)
            straight = gg_ref[:, ls].astype(F32) * sl_ref[:, ls] * skip_ref[:, ls]
            gin_ref[:, ls] = (direct + straight + back).astype(BF16)

    out_gin = pltpu.make_async_copy(gin_ref, gin_hbm.at[0], out_sems.at[2])
    out_gin.start()
    add_up(1)
    total = mine_d[pl.ds(pl.multiple_of(z * 8, 8), 8)]
    for o in range(1, depth):
        q = lax.rem(z + o, depth)
        to_level(0, q, q).wait_recv()
        total = total + zparts_d[q]
    tot_d[pl.ds(pl.multiple_of(core * HALF_D + z * 8, 8), 8)] = total
    for o in range(1, size):
        gather_d(lax.rem(me + o, size), core, z).start()
    total = mine_x[...]
    for o in range(1, depth):
        q = lax.rem(z + o, depth)
        to_level(1, q, q).wait_recv()
        total = total + zparts_x[q]
    tot_x[half_of(1, core), :] = total
    last(core).start()
    for o in range(1, size):
        j = lax.rem(me + o, size)
        gather_d(j, lax.rem(j, 2), j // 2).wait_recv()
    last(1 - core).wait_recv()

    for o in range(1, size):
        j = lax.rem(me + o, size)
        there_h(j, me).wait_send()
        there_a(j, me).wait_send()
        home_h(j, me).wait_send()
        home_a(j, me).wait_send()
    last(core).wait_send()
    for o in range(1, size):
        gather_d(lax.rem(me + o, size), core, z).wait_send()
    for p in range(2):
        for d in range(chips):
            to_sib(p, d).wait_send()
        for o in range(1, chips):
            to_chip(p, lax.rem(dp + o, chips), dp).wait_send()
        for o in range(1, depth):
            to_level(p, lax.rem(z + o, depth), z).wait_send()
    out_gated.wait()
    out_ggate.wait()
    out_gin.wait()


def finish(
    gated_in, gin_in, ggate_in, tot_d, tot_x,
    gated_out, gin_out, ggate_out, gx_ref, gdt_ref, ga_ref, gs_ref, gb_ref, gf_ref,
    hold, in_sems, out_sems,
):
    chunks = 2
    rows = T // chunks
    ins, outs = [], []
    for i, (src, dst) in enumerate(
        ((gated_in, gated_out), (gin_in, gin_out), (ggate_in, ggate_out))
    ):
        for q in range(chunks):
            at = pl.ds(q * rows, rows)
            one = i * chunks + q
            ins.append(pltpu.make_async_copy(src.at[0, at], hold.at[i, at], in_sems.at[one]))
            outs.append(pltpu.make_async_copy(hold.at[i, at], dst.at[0, at], out_sems.at[one]))
    for copy in ins:
        copy.start()
    base = RANK + N
    gx_ref[0:RANK, :] = tot_x[...]
    gx_ref[RANK:COLS, :] = tot_d[base + 8 : base + 8 + 2 * N, :]
    gdt_ref[...] = tot_d[0:RANK, :]
    ga_ref[...] = tot_d[RANK:base, :]
    gs_ref[...] = tot_d[base : base + 1, :]
    gb_ref[...] = tot_d[base + 1 : base + 2, :]
    gf_ref[...] = tot_d[base + 2 : base + 4, :]
    for into, out in zip(ins, outs):
        into.wait()
        out.start()
    for out in outs:
        out.wait()


def sds(shape, dtype=F32):
    return jax.ShapeDtypeStruct(shape, dtype)


def vm(shape, dtype=F32):
    return pltpu.VMEM(shape, dtype)


def call_step(*operands):
    dma = pltpu.SemaphoreType.DMA
    big = sds((1, T, E), BF16)
    return pl.pallas_call(
        step_kernel,
        out_shape=(big, big, big, sds((ROWS_D, 128)), sds((ROWS_X, 128))),
        in_specs=[SMEM, SMEM] + [ANY] * 9,
        out_specs=(ANY, ANY, ANY, VMEM, VMEM),
        scratch_shapes=[
            vm((T, E), BF16), vm((T, E), BF16), vm((T, E), BF16), vm((COLS, E), BF16), vm((RANK, E), BF16),
            vm((1, E)), vm((2, E)), vm((N, E)), vm((1, E)), vm((N, E)), vm((KT, N * S, 128)),
            vm((T, RANK), BF16), vm((KT, T, 128)), vm((KT, T, 128)), vm((KT, T, 128)),
            vm((L * N * S, 128)), vm((L * N * S, 128)), vm((KT, S, 128)),
            vm((KT, N * S, 128)), vm((KT, N * S, 128)),
            vm((16, 24, 128)), vm((16, 16, 128)), vm((16, 24, 128)), vm((16, 16, 128)),
            vm((16, 16, 128)), vm((16, 16, 128)), vm((16, 16, 128)), vm((16, 16, 128)),
            vm((KT * (L + 1) * N, S, 128)), vm((L * N * S, 128)), vm((L * N * S, 128)),
            vm((KT, T, 128)), vm((KT, T, 128)), vm((KT, T, 128)), vm((KT, N * S, 128)),
            vm((T, E), BF16), vm((1, T, 128)), vm((T, E)), vm((T, E)), vm((T, E)),
            vm((T, E), BF16), vm((T, E), BF16), vm((T, E), BF16),
            vm((T, 2 * N), BF16),
            vm((16, ROWS_D, 128)), vm((16, HALF_D, 128)), vm((16, HALF_D, 128)), vm((16, HALF_D, 128)),
            vm((HALF_D, 128)), vm((8, 8, 128)),
            vm((16, ROWS_X, 128)), vm((16, HALF_X, 128)), vm((16, HALF_X, 128)), vm((16, HALF_X, 128)),
            vm((HALF_X, 128)), vm((8, HALF_X, 128)),
            dma((9,)), dma((3,)), dma((4, 16)), dma((4, 16)), dma((2, 16)), dma((2, 16)),
            dma((2, 16)), dma((2, 16)), dma((2, 8)), dma((2, 8)), dma((1,)), dma((1,)),
            dma((16,)), dma((16,)),
        ],
        compiler_params=pltpu.CompilerParams(
            collective_id=0, has_side_effects=True, vmem_limit_bytes=60 << 20
        ),
        name="step_kernel",
    )(*operands)


def call_finish(*operands):
    big = sds((1, T, E), BF16)
    return pl.pallas_call(
        finish,
        out_shape=(
            big, big, big, sds((COLS, 128)), sds((RANK, 128)), sds((N, 128)), sds((1, 128)),
            sds((1, 128)), sds((2, 128)),
        ),
        in_specs=[ANY, ANY, ANY, VMEM, VMEM],
        out_specs=(ANY, ANY, ANY) + (VMEM,) * 6,
        scratch_shapes=[
            vm((3, T, E), BF16), pltpu.SemaphoreType.DMA((6,)), pltpu.SemaphoreType.DMA((6,)),
        ],
        name="finish",
    )(*operands)


def per_device(
    ssm_input, gate_input, grad_gated, x_proj, dt_proj, dt_bias, fid_bias, a_log, skip_gain,
    rec_lengths, fid_labels,
):
    results = call_step(
        rec_lengths, fid_labels, ssm_input, gate_input, grad_gated, x_proj.T, dt_proj,
        dt_bias[None, :], fid_bias, a_log.T, skip_gain[None, :],
    )
    gated, gin, ggate, gx, gdt, ga, gs, gb, gf = call_finish(*results)
    return (gated, gin, ggate, gx.T, gdt, ga.T, gs[0], gb[0], gf)


def solution(mesh):
    wide = P("dp", "seq", None)
    in_specs = (wide, wide, wide, P(), P(), P(), P(), P(), P(), P("dp"), P("dp"))
    out_specs = (
        wide, wide, wide, P("dp", None), P(None, "dp"), P("dp", None), P("dp"), P("dp"), P(None, "dp"),
    )
    return jax.shard_map(
        per_device, mesh=mesh, in_specs=in_specs, out_specs=out_specs, check_vma=False
    )
```

```python
import jax
import jax.numpy as jnp
from jax import lax
from jax.experimental import pallas as pl
from jax.experimental.pallas import tpu as pltpu
from jax.sharding import PartitionSpec as P

F32 = jnp.float32
BF16 = jnp.bfloat16
LOG2E = 1.4426950408889634
LN2 = 0.6931471805599453
T = 128
E = 2048
N = 16
RANK = 64
KT = E // 128
S = 8
L = T // S
COLS = RANK + 2 * N
ROWS_D = 128
ROWS_X = 64
HALF_D = ROWS_D // 2
HALF_X = ROWS_X // 2
MESH = pl.DeviceIdType.MESH
VMEM = pl.BlockSpec(memory_space=pltpu.VMEM)
ANY = pl.BlockSpec(memory_space=pl.ANY)
SMEM = pl.BlockSpec(memory_space=pltpu.SMEM)


def lanes(k):
    return pl.ds(pl.multiple_of(k * 128, 128), 128)


def store_permuted(ref, k, value):
    for blk in range(T // 8):
        first = (blk % 2) * 64 + blk // 2
        ref[k, pl.ds(first, 8, stride=8), :] = value[blk * 8 : blk * 8 + 8, :]


def load_natural(ref, k):
    parts = []
    for blk in range(T // 8):
        first = (blk % 2) * 64 + blk // 2
        parts.append(ref[k, pl.ds(first, 8, stride=8), :])
    return jnp.concatenate(parts, axis=0)


def sigmoid(v):
    return 1.0 / (1.0 + jnp.exp(-v))


def softplus(v):
    z = jnp.exp(-jnp.abs(v))
    r = z / (z + 2.0)
    q = r * r
    poly = 1.0 / 15.0
    for odd in (13.0, 11.0, 9.0, 7.0, 5.0, 3.0, 1.0):
        poly = poly * q + 1.0 / odd
    return jnp.maximum(v, 0.0) + 2.0 * r * poly


def live_mask(len_ref):
    t0 = lax.axis_index("seq") * T
    pos = t0 + lax.broadcasted_iota(jnp.int32, (T, 128), 0)
    return (pos < len_ref[0]).astype(F32)


def fid_row(lab_ref, fid_ref, ls):
    label = lab_ref[0]
    row = jnp.zeros((1, 128), F32)
    for kind in range(2):
        row = row + jnp.where(label == kind, fid_ref[kind : kind + 1, ls], 0.0)
    return row


def row8(ref, n, ls):
    return jnp.broadcast_to(ref[n : n + 1, ls], (8, 128))


def tile8(n):
    return pl.ds(pl.multiple_of(n * S, S), S)


def step_kernel(
    len_ref, lab_ref, u_hbm, gate_hbm, gg_hbm, xp_hbm, dtp_hbm, dtb_hbm, fid_hbm, al_hbm, skip_hbm,
    gated_hbm, gin_hbm, ggate_hbm, tot_d, tot_x,
    u_ref, gate_ref, gg_ref, xp_ref, dtp_ref, dtb_ref, fid_ref, al_ref, skip_ref, a2_ref, a2w,
    low_ref, step_ref, su_ref, gy_ref, bb_ref, cb_ref, segs_ref, hs_ref, as_ref,
    send_h, send_a, got_h, got_a, back_h, back_a, st_h, st_a,
    hbuf, bgr, cgr, ybuf, sbuf, gbuf, agbuf, dtg, dirs, sl_ref, zg_ref, ds_ref,
    gated_ref, gin_ref, ggate_ref, bcg_ref,
    grads_d, pair_d, part_d, peers_d, mine_d, zparts_d, grads_x, pair_x, part_x, peers_x, mine_x, zparts_x,
    in_sems, out_sems, x_send, x_recv, pair_send, pair_recv, chip_send, chip_recv,
    z_send, z_recv, fin_send, fin_recv, all_send, all_recv,
):
    chips = lax.axis_size("dp")
    size = lax.axis_size("seq")
    depth = size // 2
    dp = lax.axis_index("dp")
    me = lax.axis_index("seq")
    z = me // 2
    core = lax.rem(me, 2)
    sib = me + 1 - 2 * core

    loads = []
    pairs = (
        (u_hbm.at[0], u_ref), (xp_hbm, xp_ref), (dtp_hbm, dtp_ref), (dtb_hbm, dtb_ref), (fid_hbm, fid_ref),
        (gate_hbm.at[0], gate_ref), (gg_hbm.at[0], gg_ref), (al_hbm, al_ref), (skip_hbm, skip_ref),
    )
    for i, (src, dst) in enumerate(pairs):
        copy = pltpu.make_async_copy(src, dst, in_sems.at[i])
        copy.start()
        loads.append(copy)

    barrier = pltpu.get_barrier_semaphore()
    for o in range(1, chips):
        d = lax.rem(dp + o, chips)
        pl.semaphore_signal(barrier, inc=1, device_id={"dp": d}, device_id_type=MESH)
    for o in range(1, size):
        j = lax.rem(me + o, size)
        pl.semaphore_signal(barrier, inc=1, device_id={"seq": j}, device_id_type=MESH)

    def remote(src, dst, send, recv, where):
        return pltpu.make_async_remote_copy(
            src_ref=src, dst_ref=dst, send_sem=send, recv_sem=recv, device_id=where, device_id_type=MESH
        )

    def hop(which, src, dst, j, slot):
        kind = which if which < 2 else 2 * which - 2 + core
        return remote(src.at[j], dst.at[slot], x_send.at[which], x_recv.at[kind], {"seq": j})

    def bulk(ref, count, send, recv):
        some = ref.at[pl.ds(0, count)]
        return remote(some, some, send, recv, {"seq": sib})

    def there_h(j, slot):
        return hop(0, send_h, got_h, j, slot)

    def there_a(j, slot):
        return hop(1, send_a, got_a, j, slot)

    def home_h(j, slot):
        return hop(2, back_h, st_h, j, slot)

    def home_a(j, slot):
        return hop(3, back_a, st_a, j, slot)

    def group(g):
        return [2 * lax.rem(z + o, depth) + g for o in range(1, depth)]

    def send_group(copy, g, src, dst):
        for j in group(g):
            copy(j, me).start()

        @pl.when(core != g)
        def _():
            copy(sib, me).start()

        @pl.when(core == g)
        def _():
            dst[pl.ds(me, 1)] = src[pl.ds(me, 1)]

    def wait_group(which, dst, g):
        @pl.when(core != g)
        def _():
            bulk(dst, depth, x_send.at[which], x_recv.at[2 * which - 2 + g]).wait_recv()

        @pl.when(core == g)
        def _():
            bulk(dst, depth - 1, x_send.at[which], x_recv.at[2 * which - 2 + g]).wait_recv()

    grads, pair, part = (grads_d, grads_x), (pair_d, pair_x), (part_d, part_x)
    peers, mine, zparts = (peers_d, peers_x), (mine_d, mine_x), (zparts_d, zparts_x)
    halves = (HALF_D, HALF_X)

    def half_of(p, c):
        return pl.ds(pl.multiple_of(c * halves[p], 8), halves[p])

    def to_sib(p, d, turn):
        return remote(
            grads[p].at[d, half_of(p, 1 - core)], pair[p].at[d],
            pair_send.at[p], pair_recv.at[p, turn], {"seq": sib},
        )

    def to_chip(p, d, slot):
        return remote(
            part[p].at[d], peers[p].at[slot], chip_send.at[p], chip_recv.at[p], {"dp": d}
        )

    def to_level(p, q, slot):
        src = mine_x if p else mine_d.at[pl.ds(pl.multiple_of(q * 8, 8), 8)]
        return remote(
            src, zparts[p].at[slot], z_send.at[p], z_recv.at[p], {"seq": q * 2 + core}
        )

    def gather_d(j, c, q):
        here = tot_d.at[pl.ds(pl.multiple_of(c * HALF_D + q * 8, 8), 8)]
        return remote(here, here, all_send.at[0], all_recv.at[0], {"seq": j})

    def last(c):
        here = tot_x.at[half_of(1, c)]
        return remote(here, here, fin_send.at[0], fin_recv.at[0], {"seq": sib})

    loads[0].wait()
    loads[1].wait()
    proj = lax.dot_general(
        u_ref[...], xp_ref[...], (((1,), (1,)), ((), ())), preferred_element_type=F32
    )
    low_ref[...] = proj[:, :RANK].astype(BF16)
    for n in range(N):
        for col, ref in ((RANK + n, bb_ref), (RANK + N + n, cb_ref)):
            wide = jnp.broadcast_to(proj[:, col : col + 1], (T, 128))
            for blk in range(T // 8):
                first = (blk % 2) * 8 * (N * S) + n * S + blk // 2
                ref[pl.ds(first, 8, stride=N * S), :] = wide[blk * 8 : blk * 8 + 8, :]
    for copy in loads[2:]:
        copy.wait()
    a2_ref[...] = -LOG2E * jnp.exp(al_ref[...])
    live = live_mask(len_ref)

    def dt_before(ls):
        return (
            jnp.dot(low_ref[...], dtp_ref[:, ls], preferred_element_type=F32)
            + dtb_ref[:, ls]
            + fid_row(lab_ref, fid_ref, ls)
        )

    @pl.loop(0, KT // 2)
    def _(turn):
        ks = [turn * 2 + q for q in range(2)]
        raws = [dt_before(lanes(k)) for k in ks]
        for k, dt_raw in zip(ks, raws):
            ls = lanes(k)
            step = softplus(dt_raw) * live
            u = u_ref[:, ls].astype(F32)
            store_permuted(step_ref, k, step)
            store_permuted(su_ref, k, step * u)
            for n in range(N):
                a2w[k, n * S : n * S + S, :] = row8(a2_ref, n, ls)

    GK = 2
    PAIRS = KT // GK

    def tiles_of(g, q):
        return [4 * q + g, 4 * q + 2 + g]

    def zero_ends(g):
        @pl.loop(0, PAIRS // 2)
        def _(q):
            ks = tiles_of(g, q)
            GN = 8

            @pl.loop(0, N // GN)
            def _(ng):
                ns = [ng * GN + j for j in range(GN)]
                a2 = [[a2w[k, tile8(n), :] for k in ks] for n in ns]

                def ahead(tau, hh):
                    rows = tile8(tau)
                    st = [step_ref[k, rows, :] for k in ks]
                    su = [su_ref[k, rows, :] for k in ks]
                    out = []
                    for j, n in enumerate(ns):
                        b = bb_ref[tile8(tau * N + n), :]
                        for i in range(GK):
                            out.append(jnp.exp2(a2[j][i] * st[i]) * hh[j * GK + i] + b * su[i])
                    return tuple(out)

                zero = jnp.zeros((S, 128), F32)
                ends = lax.fori_loop(0, L, ahead, (zero,) * (GN * GK), unroll=16)
                for j, n in enumerate(ns):
                    for i, k in enumerate(ks):
                        hs_ref[k, tile8(n), :] = ends[j * GK + i]

        @pl.loop(0, KT // 2)
        def _(q):
            k = 2 * q + g
            seg = step_ref[k, pl.ds(0, S), :]
            for tau in range(1, L):
                seg = seg + step_ref[k, pl.ds(tau * S, S), :]
            segs_ref[k] = seg
            for nh in range(2):
                a2 = a2_ref[nh * 8 : nh * 8 + 8, lanes(k)]
                h = hs_ref[k, pl.ds(nh * 64, 8, stride=8), :]
                for s in range(1, S):
                    h = jnp.exp2(a2 * seg[s : s + 1, :]) * h + hs_ref[k, pl.ds(nh * 64 + s, 8, stride=8), :]
                send_h[k, pl.ds(nh * 8, 8), :] = h
            total = jnp.sum(seg, axis=0, keepdims=True)
            send_h[k, pl.ds(16, 8), :] = jnp.broadcast_to(total, (8, 128))

    zero_ends(0)
    pl.semaphore_wait(barrier, chips + size - 2)
    send_group(there_h, 0, send_h, got_h)
    zero_ends(1)
    send_group(there_h, 1, send_h, got_h)

    @pl.loop(0, KT // 2)
    def _(turn):
        for q in range(2):
            k = turn * 2 + q
            ls = lanes(k)
            gate = gate_ref[:, ls].astype(F32)
            sig = sigmoid(gate)
            silu = gate * sig * live
            gg = gg_ref[:, ls].astype(F32)
            sl_ref[:, ls] = silu
            zg_ref[:, ls] = gg * live * (sig * (1.0 + gate * (1.0 - sig)))
            store_permuted(gy_ref, k, gg * silu)

    def zero_pulls(g):
        @pl.loop(0, PAIRS // 2)
        def _(q):
            ks = tiles_of(g, q)
            GN = 4

            @pl.loop(0, N // GN)
            def _(ng):
                ns = [ng * GN + j for j in range(GN)]
                a2 = [[a2w[k, tile8(n), :] for k in ks] for n in ns]

                def pull(tau, state):
                    rows = tile8(tau)
                    cum = [state[i] + step_ref[k, rows, :] for i, k in enumerate(ks)]
                    gy = [gy_ref[k, rows, :] for k in ks]
                    out = list(cum)
                    for j, n in enumerate(ns):
                        c = cb_ref[tile8(tau * N + n), :]
                        for i in range(GK):
                            acc = state[GK + j * GK + i]
                            out.append(acc + jnp.exp2(a2[j][i] * cum[i]) * (c * gy[i]))
                    return tuple(out)

                zero = jnp.zeros((S, 128), F32)
                ends = lax.fori_loop(0, L, pull, (zero,) * (GK + GN * GK), unroll=16)
                for j, n in enumerate(ns):
                    for i, k in enumerate(ks):
                        as_ref[k, tile8(n), :] = ends[GK + j * GK + i]

        @pl.loop(0, KT // 2)
        def _(q):
            k = 2 * q + g
            for nh in range(2):
                a2 = a2_ref[nh * 8 : nh * 8 + 8, lanes(k)]
                h = as_ref[k, pl.ds(nh * 64 + S - 1, 8, stride=8), :]
                for s in range(S - 2, -1, -1):
                    p = jnp.exp2(a2 * segs_ref[k, s : s + 1, :])
                    h = p * h + as_ref[k, pl.ds(nh * 64 + s, 8, stride=8), :]
                send_a[k, pl.ds(nh * 8, 8), :] = h

    zero_pulls(0)
    send_group(there_a, 0, send_a, got_a)
    zero_pulls(1)
    send_group(there_a, 1, send_a, got_a)

    bgr[...] = jnp.zeros_like(bgr)
    cgr[...] = jnp.zeros_like(cgr)

    a2_mine = a2_ref[:, lanes(me)]
    bulk(got_h, size - 1, x_send.at[0], x_recv.at[0]).wait_recv()
    h = jnp.zeros((N, 128), F32)
    for i in range(size):
        back_h[i] = h
        h = jnp.exp2(a2_mine * got_h[i, 16:17, :]) * h + got_h[i, 0:16, :]
    for o in range(1, size):
        home_h(lax.rem(me + o, size), me).start()
    st_h[pl.ds(me, 1)] = back_h[pl.ds(me, 1)]

    @pl.loop(0, KT // 4)
    def _(turn):
        ks = [turn * 4 + q for q in range(4)]
        raws = [dt_before(lanes(k)) for k in ks]
        for k, dt_raw in zip(ks, raws):
            ds_ref[:, lanes(k)] = live * sigmoid(dt_raw)

    bulk(got_a, size - 1, x_send.at[1], x_recv.at[1]).wait_recv()
    g = jnp.zeros((N, 128), F32)
    for i in range(size - 1, -1, -1):
        back_a[i] = g
        g = jnp.exp2(a2_mine * got_h[i, 16:17, :]) * g + got_a[i]
    for o in range(1, size):
        home_a(lax.rem(me + o, size), me).start()
    st_a[pl.ds(me, 1)] = back_a[pl.ds(me, 1)]

    def full_forward(g):
        wait_group(2, st_h, g)

        @pl.loop(0, KT // 2)
        def _(q):
            k = 2 * q + g
            for nh in range(2):
                a2 = a2_ref[nh * 8 : nh * 8 + 8, lanes(k)]
                h = st_h[k, nh * 8 : nh * 8 + 8, :]
                for s in range(S):
                    at = pl.ds(nh * 64 + s, 8, stride=8)
                    end = hs_ref[k, at, :]
                    hs_ref[k, at, :] = h
                    if s + 1 < S:
                        h = jnp.exp2(a2 * segs_ref[k, s : s + 1, :]) * h + end

        @pl.loop(0, PAIRS // 2)
        def _(q):
            ks = tiles_of(g, q)
            kp = g * (PAIRS // 2) + q
            FN = 8
            for ng in range(N // FN):
                ns = [ng * FN + j for j in range(FN)]
                a2 = [[a2w[k, n * S : n * S + S, :] for k in ks] for n in ns]
                first = []
                for n in ns:
                    for i, k in enumerate(ks):
                        h = hs_ref[k, n * S : n * S + S, :]
                        hbuf[kp * (L + 1) * N * GK + n * GK + i] = h
                        first.append(h)

                def forward(tau, hh):
                    rows = tile8(tau)
                    st = [step_ref[k, rows, :] for k in ks]
                    su = [su_ref[k, rows, :] for k in ks]
                    gy = [gy_ref[k, rows, :] for k in ks]
                    ys = [None] * GK
                    out = []
                    for j, n in enumerate(ns):
                        at = tile8(tau * N + n)
                        b = bb_ref[at, :]
                        c = cb_ref[at, :]
                        cg = None
                        for i in range(GK):
                            h = jnp.exp2(a2[j][i] * st[i]) * hh[j * GK + i] + b * su[i]
                            out.append(h)
                            hbuf[(kp * (L + 1) + tau + 1) * (N * GK) + n * GK + i] = h
                            term = c * h
                            ys[i] = term if ys[i] is None else ys[i] + term
                            term = h * gy[i]
                            cg = term if cg is None else cg + term
                        cgr[at, :] = cgr[at, :] + cg
                    for i, k in enumerate(ks):
                        if ng == 0:
                            ybuf[k, rows, :] = ys[i]
                        else:
                            ybuf[k, rows, :] = ybuf[k, rows, :] + ys[i]
                    return tuple(out)

                lax.fori_loop(0, L, forward, tuple(first), unroll=16)

    full_forward(0)
    full_forward(1)

    def full_backward(g):
        wait_group(3, st_a, g)

        @pl.loop(0, KT // 2)
        def _(q):
            k = 2 * q + g
            for nh in range(2):
                a2 = a2_ref[nh * 8 : nh * 8 + 8, lanes(k)]
                h = st_a[k, nh * 8 : nh * 8 + 8, :]
                for s in range(S - 1, -1, -1):
                    at = pl.ds(nh * 64 + s, 8, stride=8)
                    end = as_ref[k, at, :]
                    as_ref[k, at, :] = h
                    if s > 0:
                        h = jnp.exp2(a2 * segs_ref[k, s : s + 1, :]) * h + end

        @pl.loop(0, PAIRS // 2)
        def _(q):
            ks = tiles_of(g, q)
            kp = g * (PAIRS // 2) + q
            BN = 4
            for ng in range(N // BN):
                ns = [ng * BN + j for j in range(BN)]
                a2 = [[a2w[k, n * S : n * S + S, :] for k in ks] for n in ns]
                carry = [as_ref[k, n * S : n * S + S, :] for n in ns for k in ks]
                zero = jnp.zeros((S, 128), F32)

                def behind(turn, state):
                    tau = L - 1 - turn
                    cs, ags = state
                    rows = tile8(tau)
                    st = [step_ref[k, rows, :] for k in ks]
                    su = [su_ref[k, rows, :] for k in ks]
                    gy = [gy_ref[k, rows, :] for k in ks]
                    sb = [None] * GK
                    sg = [None] * GK
                    new_c, new_a = [], []
                    for j, n in enumerate(ns):
                        at = tile8(tau * N + n)
                        b = bb_ref[at, :]
                        c = cb_ref[at, :]
                        bg = None
                        for i in range(GK):
                            g = c * gy[i] + cs[j * GK + i]
                            term = g * b
                            sb[i] = term if sb[i] is None else sb[i] + term
                            term = g * su[i]
                            bg = term if bg is None else bg + term
                            dg = jnp.exp2(a2[j][i] * st[i]) * g
                            w = dg * hbuf[(kp * (L + 1) + tau) * (N * GK) + n * GK + i]
                            term = a2[j][i] * w
                            sg[i] = term if sg[i] is None else sg[i] + term
                            new_c.append(dg)
                            new_a.append(ags[j * GK + i] + st[i] * w)
                        bgr[at, :] = bgr[at, :] + bg
                    for i, k in enumerate(ks):
                        if ng == 0:
                            sbuf[k, rows, :] = sb[i]
                            gbuf[k, rows, :] = sg[i]
                        else:
                            sbuf[k, rows, :] = sbuf[k, rows, :] + sb[i]
                            gbuf[k, rows, :] = gbuf[k, rows, :] + sg[i]
                    return tuple(new_c), tuple(new_a)

                _, ags = lax.fori_loop(0, L, behind, (tuple(carry), (zero,) * (BN * GK)), unroll=16)
                for j, n in enumerate(ns):
                    for i, k in enumerate(ks):
                        agbuf[k, n * S : n * S + S, :] = ags[j * GK + i]

    full_backward(0)
    full_backward(1)

    label = lab_ref[0]
    lane = lax.broadcasted_iota(jnp.int32, (128, 128), 1)
    sums = jnp.zeros((T, 128), F32)
    for n in range(N):
        for col, ref in ((n, bgr), (N + n, cgr)):
            tile = jnp.concatenate(
                [ref[(tau * N + n) * S : (tau * N + n) * S + S, :] for tau in range(L)], axis=0
            )
            hi = tile.astype(BF16)
            lo = (tile - hi.astype(F32)).astype(BF16)
            pick = (lane == col).astype(BF16)
            sums = sums + jnp.dot(hi, pick, preferred_element_type=F32)
            sums = sums + jnp.dot(lo, pick, preferred_element_type=F32)
    dirs[0] = sums
    bcg_ref[...] = load_natural(dirs, 0)[:, : 2 * N].astype(BF16)

    def collect(p, turn):
        bulk(pair[p], (2, 4)[p], pair_send.at[p], pair_recv.at[p, turn]).wait_recv()

    def pass_on(p, i):
        d = lax.rem(dp + 1 + i, chips)
        part[p][pl.ds(d, 1)] = grads[p][pl.ds(d, 1), half_of(p, core)] + pair[p][pl.ds(d, 1)]

    def send_on(p, i):
        pass_on(p, i)
        to_chip(p, lax.rem(dp + 1 + i, chips), dp).start()

    def early_block(i):
        k = lax.rem(dp + 1 + i, chips)
        ls = lanes(k)
        u = u_ref[:, ls]
        uf = u.astype(F32)
        step_grad = LN2 * load_natural(gbuf, k) + uf * load_natural(sbuf, k)
        dt_grad = step_grad * ds_ref[:, ls]
        dt_b = dt_grad.astype(BF16)
        dtg[:, ls] = dt_b
        grads_d[k, 0:RANK, :] = lax.dot_general(
            low_ref[...], dt_b, (((0,), (0,)), ((), ())), preferred_element_type=F32
        )
        for nh in range(2):
            ag = agbuf[k, pl.ds(nh * 64, 8, stride=8), :]
            for s in range(1, S):
                ag = ag + agbuf[k, pl.ds(nh * 64 + s, 8, stride=8), :]
            grads_d[k, RANK + nh * 8 : RANK + nh * 8 + 8, :] = (
                ag * a2_ref[nh * 8 : nh * 8 + 8, ls] * LN2
            )
        skip_row = jnp.sum(gg_ref[:, ls].astype(F32) * sl_ref[:, ls] * uf, axis=0, keepdims=True)
        dt_row = jnp.sum(dt_grad, axis=0, keepdims=True)
        zero = jnp.zeros_like(dt_row)
        base = RANK + N
        grads_d[k, base : base + 8, :] = jnp.concatenate(
            [
                skip_row,
                dt_row,
                jnp.where(label == 0, dt_row, zero),
                jnp.where(label == 1, dt_row, zero),
                zero, zero, zero, zero,
            ],
            axis=0,
        )
        grads_d[k, base + 8 : base + 8 + 2 * N, :] = lax.dot_general(
            bcg_ref[...], u, (((0,), (0,)), ((), ())), preferred_element_type=F32
        )
        grads_d[k, base + 8 + 2 * N : ROWS_D, :] = jnp.zeros((ROWS_D - base - 8 - 2 * N, 128), F32)
        return k

    def early_turn(turn):
        made = [early_block(turn * 2 + q) for q in range(2)]
        for k in made:
            to_sib(0, k, turn).start()

    early_turn(0)

    @pl.loop(1, KT // 2)
    def _(turn):
        early_turn(turn)
        collect(0, turn - 1)
        send_on(0, turn * 2 - 2)
        send_on(0, turn * 2 - 1)

    low_grad = lax.dot_general(
        dtg[...], dtp_ref[...], (((1,), (1,)), ((), ())), preferred_element_type=F32
    ).astype(BF16)
    collect(0, KT // 2 - 1)
    send_on(0, KT - 2)
    pass_on(0, KT - 1)

    def late_turn(turn):
        made = [lax.rem(dp + 1 + turn * 4 + q, chips) for q in range(4)]
        for k in made:
            grads_x[k] = lax.dot_general(
                low_grad, u_ref[:, lanes(k)], (((0,), (0,)), ((), ())), preferred_element_type=F32
            )
        for k in made:
            to_sib(1, k, turn).start()

    late_turn(0)

    @pl.loop(1, KT // 4)
    def _(turn):
        late_turn(turn)
        collect(1, turn - 1)
        for q in range(4):
            send_on(1, turn * 4 - 4 + q)

    collect(1, KT // 4 - 1)
    for q in range(3):
        send_on(1, KT - 4 + q)
    pass_on(1, KT - 1)

    def add_up(p):
        bulk(peers[p], chips - 1, chip_send.at[p], chip_recv.at[p]).wait_recv()
        total = part[p][dp]
        for o in range(1, chips):
            d = lax.rem(dp + chips - o, chips)
            total = total + peers[p][d]
        mine[p][...] = total
        for o in range(1, depth):
            to_level(p, lax.rem(z + o, depth), z).start()

    @pl.loop(0, KT // 2)
    def _(turn):
        for q in range(2):
            k = turn * 2 + q
            ls = lanes(k)
            y = load_natural(ybuf, k) + skip_ref[:, ls] * u_ref[:, ls].astype(F32)
            gated_ref[:, ls] = (y * sl_ref[:, ls]).astype(BF16)
            ggate_ref[:, ls] = (y * zg_ref[:, ls]).astype(BF16)

    out_gated = pltpu.make_async_copy(gated_ref, gated_hbm.at[0], out_sems.at[0])
    out_gated.start()
    out_ggate = pltpu.make_async_copy(ggate_ref, ggate_hbm.at[0], out_sems.at[1])
    out_ggate.start()
    add_up(0)
    proj_grad = jnp.concatenate([low_grad, bcg_ref[...]], axis=1)

    @pl.loop(0, KT // 2)
    def _(turn):
        for q in range(2):
            k = turn * 2 + q
            ls = lanes(k)
            back = jnp.dot(proj_grad, xp_ref[:, ls], preferred_element_type=F32)
            direct = load_natural(step_ref, k) * load_natural(sbuf, k)
            straight = gg_ref[:, ls].astype(F32) * sl_ref[:, ls] * skip_ref[:, ls]
            gin_ref[:, ls] = (direct + straight + back).astype(BF16)

    out_gin = pltpu.make_async_copy(gin_ref, gin_hbm.at[0], out_sems.at[2])
    out_gin.start()
    add_up(1)
    bulk(zparts_d, depth - 1, z_send.at[0], z_recv.at[0]).wait_recv()
    total = mine_d[pl.ds(pl.multiple_of(z * 8, 8), 8)]
    for o in range(1, depth):
        q = lax.rem(z + o, depth)
        total = total + zparts_d[q]
    tot_d[pl.ds(pl.multiple_of(core * HALF_D + z * 8, 8), 8)] = total
    for o in range(1, size):
        gather_d(lax.rem(me + o, size), core, z).start()
    bulk(zparts_x, depth - 1, z_send.at[1], z_recv.at[1]).wait_recv()
    total = mine_x[...]
    for o in range(1, depth):
        q = lax.rem(z + o, depth)
        total = total + zparts_x[q]
    tot_x[half_of(1, core), :] = total
    last(core).start()
    bulk(tot_d, 8 * (size - 1), all_send.at[0], all_recv.at[0]).wait_recv()
    last(1 - core).wait_recv()

    for which, src in enumerate((send_h, send_a, back_h, back_a)):
        bulk(src, size - 1, x_send.at[which], x_recv.at[0]).wait_send()
    last(core).wait_send()
    bulk(tot_d, 8 * (size - 1), all_send.at[0], all_recv.at[0]).wait_send()
    for p in range(2):
        bulk(pair[p], chips, pair_send.at[p], pair_recv.at[p, 0]).wait_send()
        bulk(part[p], chips - 1, chip_send.at[p], chip_recv.at[p]).wait_send()
        bulk(zparts[p], depth - 1, z_send.at[p], z_recv.at[p]).wait_send()
    out_gated.wait()
    out_ggate.wait()
    out_gin.wait()


def finish(
    gated_in, gin_in, ggate_in, tot_d, tot_x,
    gated_out, gin_out, ggate_out, gx_ref, gdt_ref, ga_ref, gs_ref, gb_ref, gf_ref,
    hold, in_sems, out_sems,
):
    chunks = 2
    rows = T // chunks
    ins, outs = [], []
    for i, (src, dst) in enumerate(
        ((gated_in, gated_out), (gin_in, gin_out), (ggate_in, ggate_out))
    ):
        for q in range(chunks):
            at = pl.ds(q * rows, rows)
            one = i * chunks + q
            ins.append(pltpu.make_async_copy(src.at[0, at], hold.at[i, at], in_sems.at[one]))
            outs.append(pltpu.make_async_copy(hold.at[i, at], dst.at[0, at], out_sems.at[one]))
    for copy in ins:
        copy.start()
    base = RANK + N
    gx_ref[0:RANK, :] = tot_x[...]
    gx_ref[RANK:COLS, :] = tot_d[base + 8 : base + 8 + 2 * N, :]
    gdt_ref[...] = tot_d[0:RANK, :]
    ga_ref[...] = tot_d[RANK:base, :]
    gs_ref[...] = tot_d[base : base + 1, :]
    gb_ref[...] = tot_d[base + 1 : base + 2, :]
    gf_ref[...] = tot_d[base + 2 : base + 4, :]
    for into, out in zip(ins, outs):
        into.wait()
        out.start()
    for out in outs:
        out.wait()


def sds(shape, dtype=F32):
    return jax.ShapeDtypeStruct(shape, dtype)


def vm(shape, dtype=F32):
    return pltpu.VMEM(shape, dtype)


def call_step(*operands):
    dma = pltpu.SemaphoreType.DMA
    big = sds((1, T, E), BF16)
    return pl.pallas_call(
        step_kernel,
        out_shape=(big, big, big, sds((ROWS_D, 128)), sds((ROWS_X, 128))),
        in_specs=[SMEM, SMEM] + [ANY] * 9,
        out_specs=(ANY, ANY, ANY, VMEM, VMEM),
        scratch_shapes=[
            vm((T, E), BF16), vm((T, E), BF16), vm((T, E), BF16), vm((COLS, E), BF16), vm((RANK, E), BF16),
            vm((1, E)), vm((2, E)), vm((N, E)), vm((1, E)), vm((N, E)), vm((KT, N * S, 128)),
            vm((T, RANK), BF16), vm((KT, T, 128)), vm((KT, T, 128)), vm((KT, T, 128)),
            vm((L * N * S, 128)), vm((L * N * S, 128)), vm((KT, S, 128)),
            vm((KT, N * S, 128)), vm((KT, N * S, 128)),
            vm((16, 24, 128)), vm((16, 16, 128)), vm((16, 24, 128)), vm((16, 16, 128)),
            vm((16, 16, 128)), vm((16, 16, 128)), vm((16, 16, 128)), vm((16, 16, 128)),
            vm((KT * (L + 1) * N, S, 128)), vm((L * N * S, 128)), vm((L * N * S, 128)),
            vm((KT, T, 128)), vm((KT, T, 128)), vm((KT, T, 128)), vm((KT, N * S, 128)),
            vm((T, E), BF16), vm((1, T, 128)), vm((T, E)), vm((T, E)), vm((T, E)),
            vm((T, E), BF16), vm((T, E), BF16), vm((T, E), BF16),
            vm((T, 2 * N), BF16),
            vm((16, ROWS_D, 128)), vm((16, HALF_D, 128)), vm((16, HALF_D, 128)), vm((16, HALF_D, 128)),
            vm((HALF_D, 128)), vm((8, 8, 128)),
            vm((16, ROWS_X, 128)), vm((16, HALF_X, 128)), vm((16, HALF_X, 128)), vm((16, HALF_X, 128)),
            vm((HALF_X, 128)), vm((8, HALF_X, 128)),
            dma((9,)), dma((3,)), dma((4,)), dma((6,)), dma((2,)), dma((2, 8)),
            dma((2,)), dma((2,)), dma((2,)), dma((2,)), dma((1,)), dma((1,)), dma((1,)), dma((1,)),
        ],
        compiler_params=pltpu.CompilerParams(
            collective_id=0, has_side_effects=True, vmem_limit_bytes=60 << 20
        ),
        name="step_kernel",
    )(*operands)


def call_finish(*operands):
    big = sds((1, T, E), BF16)
    return pl.pallas_call(
        finish,
        out_shape=(
            big, big, big, sds((COLS, 128)), sds((RANK, 128)), sds((N, 128)), sds((1, 128)),
            sds((1, 128)), sds((2, 128)),
        ),
        in_specs=[ANY, ANY, ANY, VMEM, VMEM],
        out_specs=(ANY, ANY, ANY) + (VMEM,) * 6,
        scratch_shapes=[
            vm((3, T, E), BF16), pltpu.SemaphoreType.DMA((6,)), pltpu.SemaphoreType.DMA((6,)),
        ],
        name="finish",
    )(*operands)


def per_device(
    ssm_input, gate_input, grad_gated, x_proj, dt_proj, dt_bias, fid_bias, a_log, skip_gain,
    rec_lengths, fid_labels,
):
    results = call_step(
        rec_lengths, fid_labels, ssm_input, gate_input, grad_gated, x_proj.T, dt_proj,
        dt_bias[None, :], fid_bias, a_log.T, skip_gain[None, :],
    )
    gated, gin, ggate, gx, gdt, ga, gs, gb, gf = call_finish(*results)
    return (gated, gin, ggate, gx.T, gdt, ga.T, gs[0], gb[0], gf)


def solution(mesh):
    wide = P("dp", "seq", None)
    in_specs = (wide, wide, wide, P(), P(), P(), P(), P(), P(), P("dp"), P("dp"))
    out_specs = (
        wide, wide, wide, P("dp", None), P(None, "dp"), P("dp", None), P("dp"), P("dp"), P(None, "dp"),
    )
    return jax.shard_map(
        per_device, mesh=mesh, in_specs=in_specs, out_specs=out_specs, check_vma=False
    )
```

```python
import jax
import jax.numpy as jnp
from jax import lax
from jax.experimental import pallas as pl
from jax.experimental.pallas import tpu as pltpu
from jax.sharding import PartitionSpec as P

F32 = jnp.float32
BF16 = jnp.bfloat16
LOG2E = 1.4426950408889634
LN2 = 0.6931471805599453
T = 128
E = 2048
N = 16
RANK = 64
KT = E // 128
S = 8
L = T // S
COLS = RANK + 2 * N
ROWS_D = 128
ROWS_X = 64
HALF_D = ROWS_D // 2
HALF_X = ROWS_X // 2
MESH = pl.DeviceIdType.MESH
VMEM = pl.BlockSpec(memory_space=pltpu.VMEM)
ANY = pl.BlockSpec(memory_space=pl.ANY)
SMEM = pl.BlockSpec(memory_space=pltpu.SMEM)


def lanes(k):
    return pl.ds(pl.multiple_of(k * 128, 128), 128)


def store_permuted(ref, k, value):
    for blk in range(T // 8):
        first = (blk % 2) * 64 + blk // 2
        ref[k, pl.ds(first, 8, stride=8), :] = value[blk * 8 : blk * 8 + 8, :]


def load_natural(ref, k):
    parts = []
    for blk in range(T // 8):
        first = (blk % 2) * 64 + blk // 2
        parts.append(ref[k, pl.ds(first, 8, stride=8), :])
    return jnp.concatenate(parts, axis=0)


def sigmoid(v):
    return 1.0 / (1.0 + jnp.exp(-v))


def softplus(v):
    z = jnp.exp(-jnp.abs(v))
    r = z / (z + 2.0)
    q = r * r
    poly = 1.0 / 15.0
    for odd in (13.0, 11.0, 9.0, 7.0, 5.0, 3.0, 1.0):
        poly = poly * q + 1.0 / odd
    return jnp.maximum(v, 0.0) + 2.0 * r * poly


def live_mask(len_ref):
    t0 = lax.axis_index("seq") * T
    pos = t0 + lax.broadcasted_iota(jnp.int32, (T, 128), 0)
    return (pos < len_ref[0]).astype(F32)


def fid_row(lab_ref, fid_ref, ls):
    label = lab_ref[0]
    row = jnp.zeros((1, 128), F32)
    for kind in range(2):
        row = row + jnp.where(label == kind, fid_ref[kind : kind + 1, ls], 0.0)
    return row


def row8(ref, n, ls):
    return jnp.broadcast_to(ref[n : n + 1, ls], (8, 128))


def tile8(n):
    return pl.ds(pl.multiple_of(n * S, S), S)


def step_kernel(
    len_ref, lab_ref, u_hbm, gate_hbm, gg_hbm, xp_hbm, dtp_hbm, dtb_hbm, fid_hbm, al_hbm, skip_hbm,
    gated_hbm, gin_hbm, ggate_hbm, tot_d, tot_x,
    u_ref, gate_ref, gg_ref, xp_ref, dtp_ref, dtb_ref, fid_ref, al_ref, skip_ref, a2_ref, a2w,
    low_ref, step_ref, su_ref, gy_ref, bb_ref, cb_ref, segs_ref, hs_ref, as_ref,
    send_h, send_a, got_h, got_a, back_h, back_a, st_h, st_a,
    hbuf, bgr, cgr, ybuf, sbuf, gbuf, agbuf, dtg, dirs, sl_ref, zg_ref, ds_ref,
    gated_ref, gin_ref, ggate_ref, bcg_ref,
    grads_d, pair_d, part_d, peers_d, mine_d, zparts_d, grads_x, pair_x, part_x, peers_x, mine_x, zparts_x,
    in_sems, out_sems, x_send, x_recv, pair_send, pair_recv, chip_send, chip_recv,
    z_send, z_recv, fin_send, fin_recv, all_send, all_recv,
):
    chips = lax.axis_size("dp")
    size = lax.axis_size("seq")
    depth = size // 2
    dp = lax.axis_index("dp")
    me = lax.axis_index("seq")
    z = me // 2
    core = lax.rem(me, 2)
    sib = me + 1 - 2 * core

    loads = []
    pairs = (
        (u_hbm.at[0], u_ref), (xp_hbm, xp_ref), (dtp_hbm, dtp_ref), (dtb_hbm, dtb_ref), (fid_hbm, fid_ref),
        (gate_hbm.at[0], gate_ref), (gg_hbm.at[0], gg_ref), (al_hbm, al_ref), (skip_hbm, skip_ref),
    )
    for i, (src, dst) in enumerate(pairs):
        copy = pltpu.make_async_copy(src, dst, in_sems.at[i])
        copy.start()
        loads.append(copy)

    barrier = pltpu.get_barrier_semaphore()
    for o in range(1, chips):
        d = lax.rem(dp + o, chips)
        pl.semaphore_signal(barrier, inc=1, device_id={"dp": d}, device_id_type=MESH)
    for o in range(1, size):
        j = lax.rem(me + o, size)
        pl.semaphore_signal(barrier, inc=1, device_id={"seq": j}, device_id_type=MESH)

    def remote(src, dst, send, recv, where):
        return pltpu.make_async_remote_copy(
            src_ref=src, dst_ref=dst, send_sem=send, recv_sem=recv, device_id=where, device_id_type=MESH
        )

    def hop(which, src, dst, j, slot):
        kind = which if which < 2 else 2 * which - 2 + core
        return remote(src.at[j], dst.at[slot], x_send.at[which], x_recv.at[kind], {"seq": j})

    def bulk(ref, count, send, recv):
        some = ref.at[pl.ds(0, count)]
        return remote(some, some, send, recv, {"seq": sib})

    def there_h(j, slot):
        return hop(0, send_h, got_h, j, slot)

    def there_a(j, slot):
        return hop(1, send_a, got_a, j, slot)

    def home_h(j, slot):
        return hop(2, back_h, st_h, j, slot)

    def home_a(j, slot):
        return hop(3, back_a, st_a, j, slot)

    def group(g):
        return [2 * lax.rem(z + o, depth) + g for o in range(1, depth)]

    def send_group(copy, g, src, dst):
        for j in group(g):
            copy(j, me).start()

        @pl.when(core != g)
        def _():
            copy(sib, me).start()

        @pl.when(core == g)
        def _():
            dst[pl.ds(me, 1)] = src[pl.ds(me, 1)]

    def wait_group(which, dst, g):
        @pl.when(core != g)
        def _():
            bulk(dst, depth, x_send.at[which], x_recv.at[2 * which - 2 + g]).wait_recv()

        @pl.when(core == g)
        def _():
            bulk(dst, depth - 1, x_send.at[which], x_recv.at[2 * which - 2 + g]).wait_recv()

    grads, pair, part = (grads_d, grads_x), (pair_d, pair_x), (part_d, part_x)
    peers, mine, zparts = (peers_d, peers_x), (mine_d, mine_x), (zparts_d, zparts_x)
    halves = (HALF_D, HALF_X)

    def half_of(p, c):
        return pl.ds(pl.multiple_of(c * halves[p], 8), halves[p])

    def to_sib(p, d, turn):
        return remote(
            grads[p].at[d, half_of(p, 1 - core)], pair[p].at[d],
            pair_send.at[p], pair_recv.at[p, turn], {"seq": sib},
        )

    def to_chip(p, d, slot):
        return remote(
            part[p].at[d], peers[p].at[slot], chip_send.at[p], chip_recv.at[p], {"dp": d}
        )

    def to_level(p, q, slot):
        src = mine_x if p else mine_d.at[pl.ds(pl.multiple_of(q * 8, 8), 8)]
        return remote(
            src, zparts[p].at[slot], z_send.at[p], z_recv.at[p], {"seq": q * 2 + core}
        )

    def gather_d(j, c, q):
        here = tot_d.at[pl.ds(pl.multiple_of(c * HALF_D + q * 8, 8), 8)]
        return remote(here, here, all_send.at[0], all_recv.at[0], {"seq": j})

    def last(c):
        here = tot_x.at[half_of(1, c)]
        return remote(here, here, fin_send.at[0], fin_recv.at[0], {"seq": sib})

    loads[0].wait()
    loads[1].wait()
    proj = lax.dot_general(
        u_ref[...], xp_ref[...], (((1,), (1,)), ((), ())), preferred_element_type=F32
    )
    low_ref[...] = proj[:, :RANK].astype(BF16)
    for n in range(N):
        for col, ref in ((RANK + n, bb_ref), (RANK + N + n, cb_ref)):
            wide = jnp.broadcast_to(proj[:, col : col + 1], (T, 128))
            for blk in range(T // 8):
                first = (blk % 2) * 8 * (N * S) + n * S + blk // 2
                ref[pl.ds(first, 8, stride=N * S), :] = wide[blk * 8 : blk * 8 + 8, :]
    for copy in loads[2:]:
        copy.wait()
    a2_ref[...] = -LOG2E * jnp.exp(al_ref[...])
    live = live_mask(len_ref)

    def dt_before(ls):
        return (
            jnp.dot(low_ref[...], dtp_ref[:, ls], preferred_element_type=F32)
            + dtb_ref[:, ls]
            + fid_row(lab_ref, fid_ref, ls)
        )

    @pl.loop(0, KT // 2)
    def _(turn):
        ks = [turn * 2 + q for q in range(2)]
        raws = [dt_before(lanes(k)) for k in ks]
        for k, dt_raw in zip(ks, raws):
            ls = lanes(k)
            step = softplus(dt_raw) * live
            u = u_ref[:, ls].astype(F32)
            store_permuted(step_ref, k, step)
            store_permuted(su_ref, k, step * u)
            for n in range(N):
                a2w[k, n * S : n * S + S, :] = row8(a2_ref, n, ls)

    GK = 2
    PAIRS = KT // GK

    def tiles_of(g, q):
        return [4 * q + g, 4 * q + 2 + g]

    def zero_ends(g):
        @pl.loop(0, PAIRS // 2)
        def _(q):
            ks = tiles_of(g, q)
            GN = 8

            @pl.loop(0, N // GN)
            def _(ng):
                ns = [ng * GN + j for j in range(GN)]
                a2 = [[a2w[k, tile8(n), :] for k in ks] for n in ns]

                def ahead(tau, hh):
                    rows = tile8(tau)
                    st = [step_ref[k, rows, :] for k in ks]
                    su = [su_ref[k, rows, :] for k in ks]
                    out = []
                    for j, n in enumerate(ns):
                        b = bb_ref[tile8(tau * N + n), :]
                        for i in range(GK):
                            out.append(jnp.exp2(a2[j][i] * st[i]) * hh[j * GK + i] + b * su[i])
                    return tuple(out)

                zero = jnp.zeros((S, 128), F32)
                ends = lax.fori_loop(0, L, ahead, (zero,) * (GN * GK), unroll=16)
                for j, n in enumerate(ns):
                    for i, k in enumerate(ks):
                        hs_ref[k, tile8(n), :] = ends[j * GK + i]

        @pl.loop(0, KT // 2)
        def _(q):
            k = 2 * q + g
            seg = step_ref[k, pl.ds(0, S), :]
            for tau in range(1, L):
                seg = seg + step_ref[k, pl.ds(tau * S, S), :]
            segs_ref[k] = seg
            for nh in range(2):
                a2 = a2_ref[nh * 8 : nh * 8 + 8, lanes(k)]
                h = hs_ref[k, pl.ds(nh * 64, 8, stride=8), :]
                for s in range(1, S):
                    h = jnp.exp2(a2 * seg[s : s + 1, :]) * h + hs_ref[k, pl.ds(nh * 64 + s, 8, stride=8), :]
                send_h[k, pl.ds(nh * 8, 8), :] = h
            total = jnp.sum(seg, axis=0, keepdims=True)
            send_h[k, pl.ds(16, 8), :] = jnp.broadcast_to(total, (8, 128))

    zero_ends(0)
    pl.semaphore_wait(barrier, chips + size - 2)
    send_group(there_h, 0, send_h, got_h)
    zero_ends(1)
    send_group(there_h, 1, send_h, got_h)

    @pl.loop(0, KT // 2)
    def _(turn):
        for q in range(2):
            k = turn * 2 + q
            ls = lanes(k)
            gate = gate_ref[:, ls].astype(F32)
            sig = sigmoid(gate)
            silu = gate * sig * live
            gg = gg_ref[:, ls].astype(F32)
            sl_ref[:, ls] = silu
            zg_ref[:, ls] = gg * live * (sig * (1.0 + gate * (1.0 - sig)))
            store_permuted(gy_ref, k, gg * silu)

    def zero_pulls(g):
        @pl.loop(0, PAIRS // 2)
        def _(q):
            ks = tiles_of(g, q)
            GN = 4

            @pl.loop(0, N // GN)
            def _(ng):
                ns = [ng * GN + j for j in range(GN)]
                a2 = [[a2w[k, tile8(n), :] for k in ks] for n in ns]

                def pull(tau, state):
                    rows = tile8(tau)
                    cum = [state[i] + step_ref[k, rows, :] for i, k in enumerate(ks)]
                    gy = [gy_ref[k, rows, :] for k in ks]
                    out = list(cum)
                    for j, n in enumerate(ns):
                        c = cb_ref[tile8(tau * N + n), :]
                        for i in range(GK):
                            acc = state[GK + j * GK + i]
                            out.append(acc + jnp.exp2(a2[j][i] * cum[i]) * (c * gy[i]))
                    return tuple(out)

                zero = jnp.zeros((S, 128), F32)
                ends = lax.fori_loop(0, L, pull, (zero,) * (GK + GN * GK), unroll=16)
                for j, n in enumerate(ns):
                    for i, k in enumerate(ks):
                        as_ref[k, tile8(n), :] = ends[GK + j * GK + i]

        @pl.loop(0, KT // 2)
        def _(q):
            k = 2 * q + g
            for nh in range(2):
                a2 = a2_ref[nh * 8 : nh * 8 + 8, lanes(k)]
                h = as_ref[k, pl.ds(nh * 64 + S - 1, 8, stride=8), :]
                for s in range(S - 2, -1, -1):
                    p = jnp.exp2(a2 * segs_ref[k, s : s + 1, :])
                    h = p * h + as_ref[k, pl.ds(nh * 64 + s, 8, stride=8), :]
                send_a[k, pl.ds(nh * 8, 8), :] = h

    zero_pulls(0)
    send_group(there_a, 0, send_a, got_a)
    zero_pulls(1)
    send_group(there_a, 1, send_a, got_a)

    bgr[...] = jnp.zeros_like(bgr)
    cgr[...] = jnp.zeros_like(cgr)

    a2_mine = a2_ref[:, lanes(me)]
    bulk(got_h, size - 1, x_send.at[0], x_recv.at[0]).wait_recv()
    h = jnp.zeros((N, 128), F32)
    for i in range(size):
        back_h[i] = h
        h = jnp.exp2(a2_mine * got_h[i, 16:17, :]) * h + got_h[i, 0:16, :]
    for o in range(1, size):
        home_h(lax.rem(me + o, size), me).start()
    st_h[pl.ds(me, 1)] = back_h[pl.ds(me, 1)]

    @pl.loop(0, KT // 4)
    def _(turn):
        ks = [turn * 4 + q for q in range(4)]
        raws = [dt_before(lanes(k)) for k in ks]
        for k, dt_raw in zip(ks, raws):
            ds_ref[:, lanes(k)] = live * sigmoid(dt_raw)

    bulk(got_a, size - 1, x_send.at[1], x_recv.at[1]).wait_recv()
    g = jnp.zeros((N, 128), F32)
    for i in range(size - 1, -1, -1):
        back_a[i] = g
        g = jnp.exp2(a2_mine * got_h[i, 16:17, :]) * g + got_a[i]
    for o in range(1, size):
        home_a(lax.rem(me + o, size), me).start()
    st_a[pl.ds(me, 1)] = back_a[pl.ds(me, 1)]

    def full_forward(g):
        wait_group(2, st_h, g)

        @pl.loop(0, KT // 2)
        def _(q):
            k = 2 * q + g
            for nh in range(2):
                a2 = a2_ref[nh * 8 : nh * 8 + 8, lanes(k)]
                h = st_h[k, nh * 8 : nh * 8 + 8, :]
                for s in range(S):
                    at = pl.ds(nh * 64 + s, 8, stride=8)
                    end = hs_ref[k, at, :]
                    hs_ref[k, at, :] = h
                    if s + 1 < S:
                        h = jnp.exp2(a2 * segs_ref[k, s : s + 1, :]) * h + end

        @pl.loop(0, PAIRS // 2)
        def _(q):
            ks = tiles_of(g, q)
            kp = g * (PAIRS // 2) + q
            FN = 8
            for ng in range(N // FN):
                ns = [ng * FN + j for j in range(FN)]
                a2 = [[a2w[k, n * S : n * S + S, :] for k in ks] for n in ns]
                first = []
                for n in ns:
                    for i, k in enumerate(ks):
                        h = hs_ref[k, n * S : n * S + S, :]
                        hbuf[kp * (L + 1) * N * GK + n * GK + i] = h
                        first.append(h)

                def forward(tau, hh):
                    rows = tile8(tau)
                    st = [step_ref[k, rows, :] for k in ks]
                    su = [su_ref[k, rows, :] for k in ks]
                    gy = [gy_ref[k, rows, :] for k in ks]
                    ys = [None] * GK
                    out = []
                    for j, n in enumerate(ns):
                        at = tile8(tau * N + n)
                        b = bb_ref[at, :]
                        c = cb_ref[at, :]
                        cg = None
                        for i in range(GK):
                            h = jnp.exp2(a2[j][i] * st[i]) * hh[j * GK + i] + b * su[i]
                            out.append(h)
                            hbuf[(kp * (L + 1) + tau + 1) * (N * GK) + n * GK + i] = h
                            term = c * h
                            ys[i] = term if ys[i] is None else ys[i] + term
                            term = h * gy[i]
                            cg = term if cg is None else cg + term
                        cgr[at, :] = cgr[at, :] + cg
                    for i, k in enumerate(ks):
                        if ng == 0:
                            ybuf[k, rows, :] = ys[i]
                        else:
                            ybuf[k, rows, :] = ybuf[k, rows, :] + ys[i]
                    return tuple(out)

                lax.fori_loop(0, L, forward, tuple(first), unroll=16)

    full_forward(0)
    full_forward(1)

    def full_backward(g):
        wait_group(3, st_a, g)

        @pl.loop(0, KT // 2)
        def _(q):
            k = 2 * q + g
            for nh in range(2):
                a2 = a2_ref[nh * 8 : nh * 8 + 8, lanes(k)]
                h = st_a[k, nh * 8 : nh * 8 + 8, :]
                for s in range(S - 1, -1, -1):
                    at = pl.ds(nh * 64 + s, 8, stride=8)
                    end = as_ref[k, at, :]
                    as_ref[k, at, :] = h
                    if s > 0:
                        h = jnp.exp2(a2 * segs_ref[k, s : s + 1, :]) * h + end

        @pl.loop(0, PAIRS // 2)
        def _(q):
            ks = tiles_of(g, q)
            kp = g * (PAIRS // 2) + q
            BN = 4
            for ng in range(N // BN):
                ns = [ng * BN + j for j in range(BN)]
                a2 = [[a2w[k, n * S : n * S + S, :] for k in ks] for n in ns]
                carry = [as_ref[k, n * S : n * S + S, :] for n in ns for k in ks]
                zero = jnp.zeros((S, 128), F32)

                def behind(turn, state):
                    tau = L - 1 - turn
                    cs, ags = state
                    rows = tile8(tau)
                    st = [step_ref[k, rows, :] for k in ks]
                    su = [su_ref[k, rows, :] for k in ks]
                    gy = [gy_ref[k, rows, :] for k in ks]
                    sb = [None] * GK
                    sg = [None] * GK
                    new_c, new_a = [], []
                    for j, n in enumerate(ns):
                        at = tile8(tau * N + n)
                        b = bb_ref[at, :]
                        c = cb_ref[at, :]
                        bg = None
                        for i in range(GK):
                            g = c * gy[i] + cs[j * GK + i]
                            term = g * b
                            sb[i] = term if sb[i] is None else sb[i] + term
                            term = g * su[i]
                            bg = term if bg is None else bg + term
                            dg = jnp.exp2(a2[j][i] * st[i]) * g
                            w = dg * hbuf[(kp * (L + 1) + tau) * (N * GK) + n * GK + i]
                            term = a2[j][i] * w
                            sg[i] = term if sg[i] is None else sg[i] + term
                            new_c.append(dg)
                            new_a.append(ags[j * GK + i] + st[i] * w)
                        bgr[at, :] = bgr[at, :] + bg
                    for i, k in enumerate(ks):
                        if ng == 0:
                            sbuf[k, rows, :] = sb[i]
                            gbuf[k, rows, :] = sg[i]
                        else:
                            sbuf[k, rows, :] = sbuf[k, rows, :] + sb[i]
                            gbuf[k, rows, :] = gbuf[k, rows, :] + sg[i]
                    return tuple(new_c), tuple(new_a)

                _, ags = lax.fori_loop(0, L, behind, (tuple(carry), (zero,) * (BN * GK)), unroll=16)
                for j, n in enumerate(ns):
                    for i, k in enumerate(ks):
                        agbuf[k, n * S : n * S + S, :] = ags[j * GK + i]

    full_backward(0)
    full_backward(1)

    label = lab_ref[0]
    lane = lax.broadcasted_iota(jnp.int32, (128, 128), 1)
    sums = jnp.zeros((T, 128), F32)
    for n in range(N):
        for col, ref in ((n, bgr), (N + n, cgr)):
            tile = jnp.concatenate(
                [ref[(tau * N + n) * S : (tau * N + n) * S + S, :] for tau in range(L)], axis=0
            )
            hi = tile.astype(BF16)
            lo = (tile - hi.astype(F32)).astype(BF16)
            pick = (lane == col).astype(BF16)
            sums = sums + jnp.dot(hi, pick, preferred_element_type=F32)
            sums = sums + jnp.dot(lo, pick, preferred_element_type=F32)
    dirs[0] = sums
    bcg_ref[...] = load_natural(dirs, 0)[:, : 2 * N].astype(BF16)

    def collect(p, turn):
        bulk(pair[p], (2, 4)[p], pair_send.at[p], pair_recv.at[p, turn]).wait_recv()

    def pass_on(p, i):
        d = lax.rem(dp + 1 + i, chips)
        part[p][pl.ds(d, 1)] = grads[p][pl.ds(d, 1), half_of(p, core)] + pair[p][pl.ds(d, 1)]

    def send_on(p, i):
        pass_on(p, i)
        to_chip(p, lax.rem(dp + 1 + i, chips), dp).start()

    def early_block(i):
        k = lax.rem(dp + 1 + i, chips)
        ls = lanes(k)
        u = u_ref[:, ls]
        uf = u.astype(F32)
        step_grad = LN2 * load_natural(gbuf, k) + uf * load_natural(sbuf, k)
        dt_grad = step_grad * ds_ref[:, ls]
        dt_b = dt_grad.astype(BF16)
        dtg[:, ls] = dt_b
        grads_d[k, 0:RANK, :] = lax.dot_general(
            low_ref[...], dt_b, (((0,), (0,)), ((), ())), preferred_element_type=F32
        )
        for nh in range(2):
            ag = agbuf[k, pl.ds(nh * 64, 8, stride=8), :]
            for s in range(1, S):
                ag = ag + agbuf[k, pl.ds(nh * 64 + s, 8, stride=8), :]
            grads_d[k, RANK + nh * 8 : RANK + nh * 8 + 8, :] = (
                ag * a2_ref[nh * 8 : nh * 8 + 8, ls] * LN2
            )
        skip_row = jnp.sum(gg_ref[:, ls].astype(F32) * sl_ref[:, ls] * uf, axis=0, keepdims=True)
        dt_row = jnp.sum(dt_grad, axis=0, keepdims=True)
        zero = jnp.zeros_like(dt_row)
        base = RANK + N
        grads_d[k, base : base + 8, :] = jnp.concatenate(
            [
                skip_row,
                dt_row,
                jnp.where(label == 0, dt_row, zero),
                jnp.where(label == 1, dt_row, zero),
                zero, zero, zero, zero,
            ],
            axis=0,
        )
        grads_d[k, base + 8 : base + 8 + 2 * N, :] = lax.dot_general(
            bcg_ref[...], u, (((0,), (0,)), ((), ())), preferred_element_type=F32
        )
        grads_d[k, base + 8 + 2 * N : ROWS_D, :] = jnp.zeros((ROWS_D - base - 8 - 2 * N, 128), F32)
        return k

    def early_turn(turn):
        made = [early_block(turn * 2 + q) for q in range(2)]
        for k in made:
            to_sib(0, k, turn).start()

    early_turn(0)

    @pl.loop(1, KT // 2)
    def _(turn):
        early_turn(turn)
        collect(0, turn - 1)
        send_on(0, turn * 2 - 2)
        send_on(0, turn * 2 - 1)

    low_grad = lax.dot_general(
        dtg[...], dtp_ref[...], (((1,), (1,)), ((), ())), preferred_element_type=F32
    ).astype(BF16)
    collect(0, KT // 2 - 1)
    send_on(0, KT - 2)
    pass_on(0, KT - 1)

    def late_turn(turn):
        made = [lax.rem(dp + 1 + turn * 4 + q, chips) for q in range(4)]
        for k in made:
            grads_x[k] = lax.dot_general(
                low_grad, u_ref[:, lanes(k)], (((0,), (0,)), ((), ())), preferred_element_type=F32
            )
        for k in made:
            to_sib(1, k, turn).start()

    late_turn(0)

    @pl.loop(1, KT // 4)
    def _(turn):
        late_turn(turn)
        collect(1, turn - 1)
        for q in range(4):
            send_on(1, turn * 4 - 4 + q)

    collect(1, KT // 4 - 1)
    for q in range(3):
        send_on(1, KT - 4 + q)
    pass_on(1, KT - 1)

    def add_up(p):
        bulk(peers[p], chips - 1, chip_send.at[p], chip_recv.at[p]).wait_recv()
        total = part[p][dp]
        for o in range(1, chips):
            d = lax.rem(dp + chips - o, chips)
            total = total + peers[p][d]
        mine[p][...] = total
        for o in range(1, depth):
            to_level(p, lax.rem(z + o, depth), z).start()

    @pl.loop(0, KT // 2)
    def _(turn):
        for q in range(2):
            k = turn * 2 + q
            ls = lanes(k)
            y = load_natural(ybuf, k) + skip_ref[:, ls] * u_ref[:, ls].astype(F32)
            gated_ref[:, ls] = (y * sl_ref[:, ls]).astype(BF16)
            ggate_ref[:, ls] = (y * zg_ref[:, ls]).astype(BF16)

    out_gated = pltpu.make_async_copy(gated_ref, gated_hbm.at[0], out_sems.at[0])
    out_gated.start()
    out_ggate = pltpu.make_async_copy(ggate_ref, ggate_hbm.at[0], out_sems.at[1])
    out_ggate.start()
    add_up(0)
    proj_grad = jnp.concatenate([low_grad, bcg_ref[...]], axis=1)

    @pl.loop(0, KT // 2)
    def _(turn):
        for q in range(2):
            k = turn * 2 + q
            ls = lanes(k)
            back = jnp.dot(proj_grad, xp_ref[:, ls], preferred_element_type=F32)
            direct = load_natural(step_ref, k) * load_natural(sbuf, k)
            straight = gg_ref[:, ls].astype(F32) * sl_ref[:, ls] * skip_ref[:, ls]
            gin_ref[:, ls] = (direct + straight + back).astype(BF16)

    out_gin = pltpu.make_async_copy(gin_ref, gin_hbm.at[0], out_sems.at[2])
    out_gin.start()
    add_up(1)
    bulk(zparts_d, depth - 1, z_send.at[0], z_recv.at[0]).wait_recv()
    total = mine_d[pl.ds(pl.multiple_of(z * 8, 8), 8)]
    for o in range(1, depth):
        q = lax.rem(z + o, depth)
        total = total + zparts_d[q]
    tot_d[pl.ds(pl.multiple_of(core * HALF_D + z * 8, 8), 8)] = total
    for o in range(1, size):
        gather_d(lax.rem(me + o, size), core, z).start()
    bulk(zparts_x, depth - 1, z_send.at[1], z_recv.at[1]).wait_recv()
    total = mine_x[...]
    for o in range(1, depth):
        q = lax.rem(z + o, depth)
        total = total + zparts_x[q]
    tot_x[half_of(1, core), :] = total
    last(core).start()
    bulk(tot_d, 8 * (size - 1), all_send.at[0], all_recv.at[0]).wait_recv()
    last(1 - core).wait_recv()

    for which, src in enumerate((send_h, send_a, back_h, back_a)):
        bulk(src, size - 1, x_send.at[which], x_recv.at[0]).wait_send()
    last(core).wait_send()
    bulk(tot_d, 8 * (size - 1), all_send.at[0], all_recv.at[0]).wait_send()
    for p in range(2):
        bulk(pair[p], chips, pair_send.at[p], pair_recv.at[p, 0]).wait_send()
        bulk(part[p], chips - 1, chip_send.at[p], chip_recv.at[p]).wait_send()
        bulk(zparts[p], depth - 1, z_send.at[p], z_recv.at[p]).wait_send()
    out_gated.wait()
    out_ggate.wait()
    out_gin.wait()


def finish(
    gated_in, gin_in, ggate_in, tot_d_in, tot_x_in,
    gated_out, gin_out, ggate_out, gx_out, gdt_out, ga_out, gs_out, gb_out, gf_out,
    hold, tot_d, tot_x, gx_ref, gdt_ref, ga_ref, gs_ref, gb_ref, gf_ref, in_sems, out_sems,
):
    small = [
        pltpu.make_async_copy(src, dst, in_sems.at[6 + i])
        for i, (src, dst) in enumerate(((tot_d_in, tot_d), (tot_x_in, tot_x)))
    ]
    for copy in small:
        copy.start()
    chunks = 2
    rows = T // chunks
    ins, outs = [], []
    for i, (src, dst) in enumerate(
        ((gated_in, gated_out), (gin_in, gin_out), (ggate_in, ggate_out))
    ):
        for q in range(chunks):
            at = pl.ds(q * rows, rows)
            one = i * chunks + q
            ins.append(pltpu.make_async_copy(src.at[0, at], hold.at[i, at], in_sems.at[one]))
            outs.append(pltpu.make_async_copy(hold.at[i, at], dst.at[0, at], out_sems.at[one]))
    for copy in ins:
        copy.start()
    for copy in small:
        copy.wait()
    base = RANK + N
    gx_ref[0:RANK, :] = tot_x[...]
    gx_ref[RANK:COLS, :] = tot_d[base + 8 : base + 8 + 2 * N, :]
    gdt_ref[...] = tot_d[0:RANK, :]
    ga_ref[...] = tot_d[RANK:base, :]
    gs_ref[...] = tot_d[base : base + 1, :]
    gb_ref[...] = tot_d[base + 1 : base + 2, :]
    gf_ref[...] = tot_d[base + 2 : base + 4, :]
    last = [
        pltpu.make_async_copy(src, dst, out_sems.at[6 + i])
        for i, (src, dst) in enumerate(
            (
                (gx_ref, gx_out), (gdt_ref, gdt_out), (ga_ref, ga_out),
                (gs_ref, gs_out), (gb_ref, gb_out), (gf_ref, gf_out),
            )
        )
    ]
    for copy in last:
        copy.start()
    for into, out in zip(ins, outs):
        into.wait()
        out.start()
    for copy in last + outs:
        copy.wait()


def sds(shape, dtype=F32):
    return jax.ShapeDtypeStruct(shape, dtype)


def vm(shape, dtype=F32):
    return pltpu.VMEM(shape, dtype)


def call_step(*operands):
    dma = pltpu.SemaphoreType.DMA
    big = sds((1, T, E), BF16)
    return pl.pallas_call(
        step_kernel,
        out_shape=(big, big, big, sds((ROWS_D, 128)), sds((ROWS_X, 128))),
        in_specs=[SMEM, SMEM] + [ANY] * 9,
        out_specs=(ANY, ANY, ANY, VMEM, VMEM),
        scratch_shapes=[
            vm((T, E), BF16), vm((T, E), BF16), vm((T, E), BF16), vm((COLS, E), BF16), vm((RANK, E), BF16),
            vm((1, E)), vm((2, E)), vm((N, E)), vm((1, E)), vm((N, E)), vm((KT, N * S, 128)),
            vm((T, RANK), BF16), vm((KT, T, 128)), vm((KT, T, 128)), vm((KT, T, 128)),
            vm((L * N * S, 128)), vm((L * N * S, 128)), vm((KT, S, 128)),
            vm((KT, N * S, 128)), vm((KT, N * S, 128)),
            vm((16, 24, 128)), vm((16, 16, 128)), vm((16, 24, 128)), vm((16, 16, 128)),
            vm((16, 16, 128)), vm((16, 16, 128)), vm((16, 16, 128)), vm((16, 16, 128)),
            vm((KT * (L + 1) * N, S, 128)), vm((L * N * S, 128)), vm((L * N * S, 128)),
            vm((KT, T, 128)), vm((KT, T, 128)), vm((KT, T, 128)), vm((KT, N * S, 128)),
            vm((T, E), BF16), vm((1, T, 128)), vm((T, E)), vm((T, E)), vm((T, E)),
            vm((T, E), BF16), vm((T, E), BF16), vm((T, E), BF16),
            vm((T, 2 * N), BF16),
            vm((16, ROWS_D, 128)), vm((16, HALF_D, 128)), vm((16, HALF_D, 128)), vm((16, HALF_D, 128)),
            vm((HALF_D, 128)), vm((8, 8, 128)),
            vm((16, ROWS_X, 128)), vm((16, HALF_X, 128)), vm((16, HALF_X, 128)), vm((16, HALF_X, 128)),
            vm((HALF_X, 128)), vm((8, HALF_X, 128)),
            dma((9,)), dma((3,)), dma((4,)), dma((6,)), dma((2,)), dma((2, 8)),
            dma((2,)), dma((2,)), dma((2,)), dma((2,)), dma((1,)), dma((1,)), dma((1,)), dma((1,)),
        ],
        compiler_params=pltpu.CompilerParams(
            collective_id=0, has_side_effects=True, vmem_limit_bytes=60 << 20
        ),
        name="step_kernel",
    )(*operands)


def call_finish(*operands):
    big = sds((1, T, E), BF16)
    return pl.pallas_call(
        finish,
        out_shape=(
            big, big, big, sds((COLS, 128)), sds((RANK, 128)), sds((N, 128)), sds((1, 128)),
            sds((1, 128)), sds((2, 128)),
        ),
        in_specs=[ANY] * 5,
        out_specs=(ANY,) * 9,
        scratch_shapes=[
            vm((3, T, E), BF16), vm((ROWS_D, 128)), vm((ROWS_X, 128)), vm((COLS, 128)), vm((RANK, 128)),
            vm((N, 128)), vm((1, 128)), vm((1, 128)), vm((2, 128)),
            pltpu.SemaphoreType.DMA((8,)), pltpu.SemaphoreType.DMA((12,)),
        ],
        name="finish",
    )(*operands)


def per_device(
    ssm_input, gate_input, grad_gated, x_proj, dt_proj, dt_bias, fid_bias, a_log, skip_gain,
    rec_lengths, fid_labels,
):
    results = call_step(
        rec_lengths, fid_labels, ssm_input, gate_input, grad_gated, x_proj.T, dt_proj,
        dt_bias[None, :], fid_bias, a_log.T, skip_gain[None, :],
    )
    gated, gin, ggate, gx, gdt, ga, gs, gb, gf = call_finish(*results)
    return (gated, gin, ggate, gx.T, gdt, ga.T, gs[0], gb[0], gf)


def solution(mesh):
    wide = P("dp", "seq", None)
    in_specs = (wide, wide, wide, P(), P(), P(), P(), P(), P(), P("dp"), P("dp"))
    out_specs = (
        wide, wide, wide, P("dp", None), P(None, "dp"), P("dp", None), P("dp"), P("dp"), P(None, "dp"),
    )
    return jax.shard_map(
        per_device, mesh=mesh, in_specs=in_specs, out_specs=out_specs, check_vma=False
    )
```
